32 devices in a mesh: tm: 4 (over y, x), space: 8 (over z, core).
Axes of the slice: x: 2, y: 2, z: 4, core: 2. Of those that a mesh axis runs over, the one named last changes fastest.
Arguments:
- source: float32 [16, 32, 96, 128], P('tm', 'space'), may hold values from -6 to 6
- initial: float32 [32, 96, 128], P('space'), may hold values from -6 to 6
- mobility: float32 [32, 96, 128], P('space'), may hold values from 0.5 to 2
- labels: int32 [32, 96, 128], P('space'), may hold values from 0 to 3
- electrode: int32 [32, 96, 128], P('space'), may hold values 0 or 1
- rates: float32 [4], replicated, may hold values from 0.2 to 1
Outputs:
- density: float32 [16, 32, 96, 128], P('tm', 'space')
The draws below stay inside these ranges and needn't reach their ends.
All inputs are finite; a program needn't handle non-finite values. No bound on the sum of `electrode` on one device may be relied on, other than what follows from the above.
Results may differ from the reference program's by a relative error of at most 0.00002.
Values sent between devices are 32-bit elements; how exact they have to be, the bound alone decides.
A program may use at most 64 MiB of HBM per device.

```python
import math
import jax
import jax.numpy as jnp
from jax import lax

TS = 4
NY = 96
NZ = 128
PASSES = 4
PRE = 1
POST = 1
REGIONS = 4
NT = 16
NX = 32
N_TM = 4


def touch_ends(array, rng, least, high):
    longest = array.shape.index(max(array.shape))
    spots = []
    for shift in (0, 1):
        where = [jax.random.randint(jax.random.fold_in(rng, axis), (), 0, length) for axis, length in enumerate(array.shape)]
        where[longest] = (where[longest] + shift) % array.shape[longest]
        spots.append(tuple(where))
    return array.at[spots[0]].set(least).at[spots[1]].set(high)


def shard_levels(rng, dims, cuts, smallest, largest):
    def one(dim, parts):
        draws = jax.random.uniform(jax.random.fold_in(jax.random.fold_in(rng, 6), dim), (parts,), jnp.float32, smallest / len(cuts), largest / len(cuts))
        return jnp.repeat(jnp.exp(draws), dims[dim] // parts).reshape((-1,) + (1,) * (len(dims) - dim - 1))

    factor_of = one(*cuts[0])
    for cut in cuts[1:]:
        factor_of = factor_of * one(*cut)
    return factor_of


def normal_values(own_key, dims, width, reach, cuts=(), kind=jnp.bfloat16):
    result = jax.random.normal(own_key, dims, jnp.float32) * width
    if len(cuts) > 0:
        result = shard_levels(own_key, dims, cuts, -0.22, 0.18) * result
    return jnp.clip(result, min=-reach, max=reach).astype(kind)


def setup_inputs(seed: int = 0) -> dict:
    key_list = jax.random.split(jax.random.key(seed), 7)
    return {
        "source": normal_values(key_list[0], (NT, NX, NY, NZ), 1.0, 6.0, ((0, 4), (1, 8)), jnp.float32),
        "initial": normal_values(key_list[1], (NX, NY, NZ), 1.0, 6.0, ((0, 8),), jnp.float32),
        "mobility": jnp.clip(jnp.exp(math.log(2.0) - 1.3862944 * jax.random.uniform(key_list[2], (NX, NY, NZ), jnp.float32) ** shard_levels(key_list[2], (NX, NY, NZ), ((0, 8),), -0.2, 0.2)), 0.5, 2.0),
        "labels": touch_ends(jax.random.randint(key_list[3], (NX, NY, NZ), 0, REGIONS), jax.random.fold_in(key_list[3], 1), 0, REGIONS - 1).astype(jnp.int32),
        "electrode": touch_ends((jax.random.randint(key_list[4], (NX, NY, NZ), 0, 8) < 1).astype(jnp.int32), jax.random.fold_in(key_list[4], 1), 0, 1),
        "rates": jnp.clip(jnp.exp(jax.random.uniform(key_list[5], (REGIONS,), jnp.float32, math.log(0.2), math.log(1.0))), 0.2, 1.0),
    }


source_coef = 0.5
drift_coef = 0.5
react_coef = 0.5
damping = 0.8
coarse_lateral = 0.06
coarse_axial = 0.12


def pad_across(values):
    return jnp.pad(values, ((0, 0), (0, 0), (1, 1), (1, 1)))


def balance(window, mobile, rate_field, forcing):
    current = window[1:, 1:-1]
    former = window[:-1, 1:-1]
    middle = mobile[:, 1:-1]
    spread = pad_across(middle)
    below_x = 0.5 * (middle + mobile[:, :-2])
    above_x = 0.5 * (middle + mobile[:, 2:])
    below_y = 0.5 * (middle + spread[:, :, :-2, 1:-1])
    above_y = 0.5 * (middle + spread[:, :, 2:, 1:-1])
    below_z = 0.5 * (middle + spread[:, :, 1:-1, :-2])
    above_z = 0.5 * (middle + spread[:, :, 1:-1, 2:])
    beside_all = pad_across(current)
    lower_z = beside_all[:, :, 1:-1, :-2]
    summed = below_x + above_x + below_y + above_y + below_z + above_z
    inflow = (below_x * window[1:, :-2] + above_x * window[1:, 2:]
              + below_y * beside_all[:, :, :-2, 1:-1] + above_y * beside_all[:, :, 2:, 1:-1]
              + below_z * lower_z + above_z * beside_all[:, :, 1:-1, 2:] - summed * current)
    carried = below_z * lower_z - above_z * current
    magnitude = jnp.abs(current)
    excess = current - former - inflow - drift_coef * carried + react_coef * rate_field * current * magnitude
    residue = forcing - excess
    diagonal = 1.0 + summed + drift_coef * above_z + rate_field * magnitude
    return residue, diagonal, current


def relax(window, mobile, rate_field, freedom, forcing):
    residue, diagonal, current = balance(window, mobile, rate_field, forcing)
    updated = current + damping * freedom * residue / diagonal
    return jnp.concatenate([window[:1, 1:-1], updated], axis=0)


def coarse_change(extended, mobility_ext):
    centre = extended[1:-1, 1:-1]
    centre_mob = mobility_ext[1:-1, 1:-1]
    padded_value = jnp.pad(centre, ((0, 0), (0, 0), (1, 1)))
    padded_mob = jnp.pad(centre_mob, ((0, 0), (0, 0), (1, 1)))

    def couple(value_near, mobile_near):
        return 0.5 * (centre_mob + mobile_near) * (value_near - centre)

    lateral = (couple(extended[:-2, 1:-1], mobility_ext[:-2, 1:-1])
               + couple(extended[2:, 1:-1], mobility_ext[2:, 1:-1])
               + couple(extended[1:-1, :-2], mobility_ext[1:-1, :-2])
               + couple(extended[1:-1, 2:], mobility_ext[1:-1, 2:]))
    along_z = couple(padded_value[:, :, :-2], padded_mob[:, :, :-2]) + couple(padded_value[:, :, 2:], padded_mob[:, :, 2:])
    return centre + coarse_lateral * lateral + coarse_axial * along_z


def region_rates(labels, rates):
    matches = labels[None] == jnp.arange(rates.shape[0], dtype=jnp.int32)[:, None, None, None]
    return jnp.sum(jnp.where(matches, rates[:, None, None, None], 0.0), axis=0)


def restrict(residue):
    step_count, planes, across, depth_z = residue.shape
    grouped = residue.reshape(step_count // 4, 4, planes // 2, 2, across // 2, 2, depth_z)
    return 0.25 * jnp.sum(grouped, axis=(1, 3, 5))


def coarse_mobility(mobility):
    planes, across, depth_z = mobility.shape
    return 0.25 * jnp.sum(mobility.reshape(planes // 2, 2, across // 2, 2, depth_z), axis=(1, 3))


def prolong(correction):
    return jnp.repeat(jnp.repeat(jnp.repeat(correction, 4, axis=0), 2, axis=1), 2, axis=2)


def reference(source, initial, mobility, labels, electrode, rates):
    rate_field = region_rates(labels, rates)[None]
    freedom = (1.0 - electrode.astype(jnp.float32))[None]
    forcing = source_coef * source
    padded_mob = jnp.pad(mobility, ((1, 1), (0, 0), (0, 0)))[None]
    layout = (N_TM, TS) + initial.shape
    forcing_blocks = forcing.reshape(layout)

    def pad_planes(window):
        return jnp.pad(window, ((0, 0), (1, 1), (0, 0), (0, 0)))

    def windows(iterate):
        blocks = iterate.reshape(layout)
        before = jnp.concatenate([initial[None], blocks[:-1, -1]], axis=0)
        return blocks, before

    def sweep(iterate):
        blocks, before = windows(iterate)

        def per_block(members):
            time_block, opening, pushed = members
            window = jnp.concatenate([opening[None], time_block], axis=0)
            for number in range(PASSES):
                window = relax(pad_planes(window), padded_mob, rate_field, freedom, pushed)
            return window[1:]

        return lax.map(per_block, (blocks, before, forcing_blocks)).reshape(iterate.shape)

    def residual_of(iterate):
        blocks, before = windows(iterate)

        def per_block(members):
            time_block, opening, pushed = members
            window = jnp.concatenate([opening[None], time_block], axis=0)
            return balance(pad_planes(window), padded_mob, rate_field, pushed)[0]

        return lax.map(per_block, (blocks, before, forcing_blocks)).reshape(iterate.shape)

    iterate = jnp.broadcast_to(initial, source.shape)
    for number in range(PRE):
        iterate = sweep(iterate)
    coarse_rhs = restrict(residual_of(iterate))
    mob_ext = jnp.pad(coarse_mobility(mobility), ((1, 1), (1, 1), (0, 0)))

    def advance(carry_state, forcing_row):
        advanced = coarse_change(jnp.pad(carry_state, ((1, 1), (1, 1), (0, 0))), mob_ext) + forcing_row
        return advanced, advanced

    final_state, history = lax.scan(advance, jnp.zeros(coarse_rhs.shape[1:], jnp.float32), coarse_rhs)
    iterate = iterate + freedom * prolong(history)
    for number in range(POST):
        iterate = sweep(iterate)
    return iterate
```

```python
import functools

import jax
import jax.numpy as jnp
from jax import lax
from jax.experimental import pallas as pl
from jax.experimental.pallas import tpu as pltpu
from jax.sharding import PartitionSpec as P

PASSES = 4

source_coef = 0.5
drift_coef = 0.5
react_coef = 0.5
damping = 0.8
coarse_lateral = 0.06
coarse_axial = 0.12

PAD = 8


def kernel(
    n_tm,
    n_space,
    regions,
    source,
    initial,
    mobility,
    labels,
    electrode,
    rates,
    out,
    V,
    IE,
    ME,
    EB,
    F,
    FS,
    KP,
    FR,
    FW,
    FX,
    FY,
    BZ,
    AZ,
    D0,
    W,
    TMP,
    HS,
    HX,
    OS,
    OB,
    VO,
    CM,
    GX,
    GY,
    GL,
    GH,
    GD,
    R,
    C,
    UP,
    s_init,
    r_init,
    s_v,
    r_v,
    s_cm,
    r_cm,
    s_hx,
    r_hx,
    s_o,
    r_o,
    s_r,
    r_r,
    s_d,
    r_d,
    s_vo,
    r_vo,
):
    T, X, Y, Z = source.shape
    A, YC = X // 2, Y // 2
    H = -(-n_tm // A)
    E = A * H
    CP = A + 2 * E
    rows = pl.ds(PAD, Y)
    crows = pl.ds(PAD, YC)
    k = lax.axis_index("tm")
    s = lax.axis_index("space")

    def beyond(q, d=1):
        return s >= d if q == 0 else s + d < n_space

    def space_id(q, d=1):
        return {"space": s - d if q == 0 else s + d}

    def remote(src, dst, send, recv, where):
        return pltpu.make_async_remote_copy(
            src_ref=src,
            dst_ref=dst,
            send_sem=send,
            recv_sem=recv,
            device_id=where,
            device_id_type=pl.DeviceIdType.MESH,
        )

    def each_side(action, d=1):
        for q in (0, 1):
            pl.when(beyond(q, d))(functools.partial(action, q))

    barrier = pltpu.get_barrier_semaphore()

    def greet(where):
        pl.semaphore_signal(
            barrier, inc=1, device_id=where, device_id_type=pl.DeviceIdType.MESH
        )

    for d in range(1, H + 1):
        each_side(lambda q, d=d: greet(space_id(q, d)), d)
    for d in range(1, n_tm):
        greet({"tm": lax.rem(k + d, n_tm)})

    edge = jnp.zeros((PAD, Z), jnp.float32)
    plane = jnp.zeros((Y, Z), jnp.float32)
    cplane = jnp.zeros((YC, Z), jnp.float32)
    top, bottom = pl.ds(0, PAD), pl.ds(PAD + Y, PAD)
    ctop, cbottom = pl.ds(0, PAD), pl.ds(PAD + YC, PAD)
    for x in range(X + 2):
        for ref in (IE, ME, W):
            ref[x, top] = edge
            ref[x, bottom] = edge

        def clear(i, carry, x=x):
            for b in (0, 1):
                V[b, i, x, top] = edge
                V[b, i, x, bottom] = edge
            return carry

        lax.fori_loop(1, T + 1, clear, 0)
    for x in range(X):
        FY[x, bottom] = edge
        IE[x + 1, rows] = initial[x]
        ME[x + 1, rows] = mobility[x]
        for b in (0, 1):
            V[b, 0, x + 1, rows] = initial[x]
    W[0, rows] = plane
    W[X + 1, rows] = plane

    def clear_coarse(p, carry):
        for ref in (CM, GY):
            ref[p, ctop] = edge
            ref[p, cbottom] = edge
        for j in range(n_tm):
            C[j, p, ctop] = edge
            C[j, p, cbottom] = edge
        return carry

    lax.fori_loop(0, CP, clear_coarse, 0)
    for q in (0, 1):

        @pl.when(jnp.logical_not(beyond(q)))
        def _(q=q):
            x = 0 if q == 0 else X + 1
            IE[x, rows] = plane
            ME[x, rows] = plane
            FR[x] = plane
            HX[q] = cplane

            def clear_halo(i, carry):
                for b in (0, 1):
                    V[b, i, x, rows] = plane
                return carry

            lax.fori_loop(1, T + 1, clear_halo, 0)

        for d in range(1, H + 1):

            @pl.when(jnp.logical_not(beyond(q, d)))
            def _(q=q, d=d):
                for a in range(A):
                    p = E - A * d + a if q == 0 else E + A * d + a
                    CM[p, crows] = cplane
                    for j in range(n_tm):
                        R[j, p] = cplane

    peers = jnp.minimum(s, H) + jnp.minimum(n_space - 1 - s, H) + (n_tm - 1)
    pl.semaphore_wait(barrier, peers)

    def start_copy(item, q):
        src, dst = ((initial, IE), (mobility, ME), (electrode, EB))[item]
        x = 0 if q == 0 else X - 1
        if item < 2:
            target = dst.at[X + 1 if q == 0 else 0, rows]
        else:
            target = dst.at[1 - q]
        return remote(src.at[x], target, s_init.at[item, q], r_init.at[item, 1 - q], space_id(q))

    def landed(item, q):
        src, dst = ((initial, IE), (mobility, ME), (electrode, EB))[item]
        if item < 2:
            target = dst.at[0 if q == 0 else X + 1, rows]
        else:
            target = dst.at[q]
        return remote(src.at[0], target, s_init.at[item, q], r_init.at[item, q], space_id(q))

    for item in (1, 0, 2):
        each_side(lambda q, item=item: start_copy(item, q).start())

    def pair_rows(value, slot):
        TMP[slot] = value
        return TMP[slot, pl.ds(0, YC, stride=2), :] + TMP[slot, pl.ds(1, YC, stride=2), :]

    for a in range(A):
        CM[E + a, crows] = 0.25 * pair_rows(mobility[2 * a] + mobility[2 * a + 1], a)

    def reach(j, d):
        return min(A, n_tm - j - A * (d - 1))

    def deep(ref, pick, j, q, d, send, recv, incoming):
        n = reach(j, d)
        mine = E if q == 0 else E + A - n
        if incoming:
            there = E - A * d + A - n if q == 0 else E + A * d
        else:
            there = E + A * d if q == 0 else E - A * d + A - n
        slot = 2 * (d - 1)
        return remote(
            pick(ref, mine, n),
            pick(ref, there, n),
            send(slot + q),
            recv(slot + (q if incoming else 1 - q)),
            space_id(q, d),
        )

    def cm_copy(q, d, incoming):
        return deep(
            CM,
            lambda ref, p, n: ref.at[pl.ds(p, n), crows],
            0,
            q,
            d,
            lambda i: s_cm.at[i],
            lambda i: r_cm.at[i],
            incoming,
        )

    for d in range(1, H + 1):
        each_side(lambda q, d=d: cm_copy(q, d, False).start(), d)

    lane = lax.broadcasted_iota(jnp.int32, (Y, Z), 1)
    not_first, not_last = lane > 0, lane < Z - 1

    def half_forcing(t, carry):
        for x in range(X):
            F[t, x] = source_coef * source[t, x]
        return carry

    lax.fori_loop(0, T, half_forcing, 0)
    for x in range(X):
        total = F[0, x]
        for t in range(1, T):
            total = total + F[t, x]
        FS[x] = total
        lab = labels[x]
        rate = jnp.zeros((Y, Z), jnp.float32)
        for i in range(regions):
            rate = jnp.where(lab == i, rates[i], rate)
        KP[x] = rate
        free = 1.0 - electrode[x].astype(jnp.float32)
        FR[x + 1] = free
        FW[x] = damping * free
        mid = mobility[x]
        FY[x, rows] = 0.5 * (mid + ME[x + 1, pl.ds(PAD - 1, Y)])
        FY[x, pl.ds(PAD + Y, 1)] = 0.5 * mobility[x, pl.ds(Y - 1, 1)]
        low = 0.5 * (mid + jnp.where(not_first, pltpu.roll(mid, 1, 1), 0.0))
        high = 0.5 * (mid + jnp.where(not_last, pltpu.roll(mid, Z - 1, 1), 0.0))
        BZ[x] = jnp.where(not_first, (1.0 + drift_coef) * low, 0.0)
        AZ[x] = jnp.where(not_last, high, 0.0)
        D0[x] = 1.0 + low + (1.0 + drift_coef) * high + FY[x, rows] + FY[x, pl.ds(PAD + 1, Y)]
    for x in range(1, X):
        FX[x] = 0.5 * (mobility[x - 1] + mobility[x])

    @pl.when(k == 0)
    def _():
        for a in range(A):
            OB[a] = pair_rows(initial[2 * a] + initial[2 * a + 1], a)

    each_side(lambda q: landed(1, q).wait_recv())
    FX[0] = 0.5 * (ME[0, rows] + ME[1, rows])
    FX[X] = 0.5 * (ME[X, rows] + ME[X + 1, rows])
    for x in range(X):
        D0[x] = D0[x] + FX[x] + FX[x + 1]

    def around(read, x, centre):
        i = x - 1
        return (
            FX[i] * read(x - 1, PAD)
            + FX[i + 1] * read(x + 1, PAD)
            + FY[i, rows] * read(x, PAD - 1)
            + FY[i, pl.ds(PAD + 1, Y)] * read(x, PAD + 1)
            + BZ[i] * pltpu.roll(centre, 1, 1)
            + AZ[i] * pltpu.roll(centre, Z - 1, 1)
        )

    def v_copy(b, t, q):
        x = 1 if q == 0 else X
        there = X + 1 if q == 0 else 0
        return remote(
            V.at[b, t + 1, x, rows],
            V.at[b, t + 1, there, rows],
            s_v.at[b, q, t],
            r_v.at[b, 1 - q, t],
            space_id(q),
        )

    def v_landed(b, t, q):
        x = 0 if q == 0 else X + 1
        return remote(
            V.at[b, t + 1, 1, rows],
            V.at[b, t + 1, x, rows],
            s_v.at[b, q, t],
            r_v.at[b, q, t],
            space_id(q),
        )

    each_side(lambda q: landed(0, q).wait_recv())

    def first_plane(x):
        i = x - 1
        now = IE[x, rows]
        pull = KP[i] * jnp.abs(now)
        diag = D0[i] + pull
        common = around(lambda xx, o: IE[xx, pl.ds(o, Y)], x, now) + now - now * (
            diag - react_coef * pull
        )
        TMP[0] = common
        TMP[1] = FW[i] / diag

        def step(t, carry):
            V[1, t + 1, x, rows] = IE[x, rows] + TMP[1] * (F[t, i] + TMP[0])
            if x in (1, X):
                q = 0 if x == 1 else 1
                pl.when(beyond(q))(lambda: v_copy(1, t, q).start())
            return carry

        lax.fori_loop(0, T, step, 0)

    for x in (1, X) + tuple(range(2, X)):
        first_plane(x)

    def relaxed(b, t, x):
        i = x - 1
        now = V[b, t + 1, x, rows]
        pull = KP[i] * jnp.abs(now)
        diag = D0[i] + pull
        gain = (
            F[t, i]
            + V[b, t, x, rows]
            + around(lambda xx, o: V[b, t + 1, xx, pl.ds(o, Y)], x, now)
            - now * (diag - react_coef * pull)
        )
        return now + FW[i] * gain / diag

    def one_pass(b, arriving, sending, free_send, last):
        o = 1 - b

        def store(t, x, value):
            if last:
                out[t, x - 1] = value
            else:
                V[o, t + 1, x, rows] = value

        def ends(t, carry):
            if arriving:
                each_side(lambda q: v_landed(b, t, q).wait_recv())
            if free_send:
                each_side(lambda q: v_copy(o, t, q).wait_send())
            for q, x in ((0, 1), (1, X)):
                store(t, x, relaxed(b, t, x))
                if sending:
                    pl.when(beyond(q))(functools.partial(lambda q: v_copy(o, t, q).start(), q))
            return carry

        def inner(t, carry):
            for x in range(2, X):
                store(t, x, relaxed(b, t, x))
            return carry

        lax.fori_loop(0, T, ends, 0)
        lax.fori_loop(0, T, inner, 0)

    for number in range(2, PASSES + 1):
        one_pass((number + 1) % 2, True, number < PASSES, number > 2, False)
    g = PASSES % 2

    def total_of(x):
        total = V[g, 1, x, rows]
        for t in range(1, T):
            total = total + V[g, t + 1, x, rows]
        return total

    def hx_copy(q):
        return remote(HS.at[q], HX.at[1 - q], s_hx.at[q], r_hx.at[1 - q], space_id(q))

    def hx_landed(q):
        return remote(HS.at[q], HX.at[q], s_hx.at[q], r_hx.at[q], space_id(q))

    for q, x in ((0, 1), (1, X)):
        total = total_of(x)
        W[x, rows] = total
        HS[q] = 0.25 * pair_rows(FX[0 if q == 0 else X] * total, q)
        pl.when(beyond(q))(functools.partial(lambda q: hx_copy(q).start(), q))

    o_copy = remote(OS, OB, s_o, r_o, {"tm": lax.rem(k + 1, n_tm)})
    for a in range(A):
        OS[a] = pair_rows(V[g, T, 2 * a + 1, rows] + V[g, T, 2 * a + 2, rows], a)

    @pl.when(k < n_tm - 1)
    def _():
        o_copy.start()

    def v_out(t, carry):
        each_side(lambda q: v_copy(g, t, q).start())
        return carry

    lax.fori_loop(0, T, v_out, 0)

    for x in range(2, X):
        W[x, rows] = total_of(x)

    def residual_sum(x):
        i = x - 1
        total = W[x, rows]
        quad = jnp.zeros((Y, Z), jnp.float32)
        for t in range(T):
            value = V[g, t + 1, x, rows]
            quad = quad + value * jnp.abs(value)
        return (
            FS[i]
            + (total - V[g, T, x, rows])
            + around(lambda xx, o: W[xx, pl.ds(o, Y)], x, total)
            - D0[i] * total
            - react_coef * KP[i] * quad
        )

    own = []
    for a in range(A):
        own.append(pair_rows(residual_sum(2 * a + 1) + residual_sum(2 * a + 2), a))

    @pl.when(k > 0)
    def _():
        o_copy.wait_recv()

    each_side(lambda q: hx_landed(q).wait_recv())
    for a in range(A):
        value = 0.25 * (own[a] + OB[a])
        if a == 0:
            value = value + HX[0]
        if a == A - 1:
            value = value + HX[1]
        R[k, E + a] = value

    def r_copy(d):
        return remote(
            R.at[k, pl.ds(E, A)],
            R.at[k, pl.ds(E, A)],
            s_r.at[d],
            r_r.at[k],
            {"tm": lax.rem(k + d, n_tm)},
        )

    def r_landed(j):
        return remote(
            R.at[j, pl.ds(E, A)],
            R.at[j, pl.ds(E, A)],
            s_r.at[0],
            r_r.at[j],
            {"tm": lax.rem(k + 1, n_tm)},
        )

    for d in range(n_tm - 1, 0, -1):
        r_copy(d).start()

    vo_copy = remote(
        V.at[g, T, pl.ds(1, X), rows], VO, s_vo, r_vo, {"tm": lax.rem(k + 1, n_tm)}
    )

    @pl.when(k < n_tm - 1)
    def _():
        vo_copy.start()

    for d in range(1, H + 1):
        each_side(lambda q, d=d: cm_copy(q, d, True).wait_recv(), d)
    clane = lax.broadcasted_iota(jnp.int32, (YC, Z), 1)
    c_first, c_last = clane > 0, clane < Z - 1
    lo = E - (n_tm - 1)
    hi = E + A + (n_tm - 1)

    def coarse_faces(p, carry):
        GX[p] = (0.5 * coarse_lateral) * (CM[p - 1, crows] + CM[p, crows])
        return carry

    lax.fori_loop(lo, hi + 1, coarse_faces, 0)

    def coarse_coefs(p, carry):
        mid = CM[p, crows]
        near = (0.5 * coarse_lateral) * (mid + CM[p, pl.ds(PAD - 1, YC)])
        far = (0.5 * coarse_lateral) * (mid + CM[p, pl.ds(PAD + 1, YC)])
        GY[p, crows] = near
        low = (0.5 * coarse_axial) * (
            mid + jnp.where(c_first, pltpu.roll(mid, 1, 1), 0.0)
        )
        high = (0.5 * coarse_axial) * (
            mid + jnp.where(c_last, pltpu.roll(mid, Z - 1, 1), 0.0)
        )
        GL[p] = jnp.where(c_first, low, 0.0)
        GH[p] = jnp.where(c_last, high, 0.0)
        GD[p] = 1.0 - (GX[p] + GX[p + 1] + near + far + low + high)
        return carry

    lax.fori_loop(lo, hi, coarse_coefs, 0)

    def d_copy(j, q, d, incoming):
        return deep(
            R,
            lambda ref, p, n: ref.at[j, pl.ds(p, n)],
            j,
            q,
            d,
            lambda i: s_d.at[j, i],
            lambda i: r_d.at[j, i],
            incoming,
        )

    def distances(j):
        return [d for d in range(1, H + 1) if reach(j, d) > 0]

    for j in range(n_tm):
        pl.when(k != j)(lambda j=j: r_landed(j).wait_recv())
        for d in distances(j):
            each_side(lambda q, d=d, j=j: d_copy(j, q, d, False).start(), d)

    for j in range(n_tm):
        for d in distances(j):
            each_side(lambda q, d=d, j=j: d_copy(j, q, d, True).wait_recv(), d)

        def coarse_plane(p, carry, j=j):
            if j == 0:
                C[0, p, crows] = R[0, p]
                return carry
            mid = C[j - 1, p, crows]
            value = (
                R[j, p]
                + GD[p] * mid
                + GX[p] * C[j - 1, p - 1, crows]
                + GX[p + 1] * C[j - 1, p + 1, crows]
                + GY[p, crows] * C[j - 1, p, pl.ds(PAD - 1, YC)]
                + GY[p, pl.ds(PAD + 1, YC)] * C[j - 1, p, pl.ds(PAD + 1, YC)]
                + GL[p] * pltpu.roll(mid, 1, 1)
                + GH[p] * pltpu.roll(mid, Z - 1, 1)
            )
            where = A * s + p - E
            inside = jnp.logical_and(where >= 0, where < A * n_space)
            C[j, p, crows] = jnp.where(inside, value, 0.0)
            return carry

        width = n_tm - j
        lax.fori_loop(E - width, E + A + width, coarse_plane, 0)

    each_side(lambda q: landed(2, q).wait_recv())
    for q in (0, 1):

        @pl.when(beyond(q))
        def _(q=q):
            FR[0 if q == 0 else X + 1] = 1.0 - EB[q].astype(jnp.float32)

    def spread(j, x):
        value = C[j, E + (x + 1) // 2 - 1, crows]
        UP[x, pl.ds(0, YC, stride=2), :] = value
        UP[x, pl.ds(1, YC, stride=2), :] = value
        return FR[x] * UP[x]

    def v_home(t, carry):
        each_side(lambda q: v_copy(g, t, q).wait_send())
        each_side(lambda q: v_landed(g, t, q).wait_recv())
        return carry

    lax.fori_loop(0, T, v_home, 0)

    @pl.when(k < n_tm - 1)
    def _():
        vo_copy.wait_send()

    for x in range(X + 2):
        move = spread(k, x)
        for t in range(T):
            V[g, t + 1, x, rows] = V[g, t + 1, x, rows] + move

    @pl.when(k > 0)
    def _():
        vo_copy.wait_recv()
        for x in range(1, X + 1):
            opening = VO[x - 1] + spread(k - 1, x)
            for b in (0, 1):
                V[b, 0, x, rows] = opening

    for number in range(1, PASSES + 1):
        one_pass(
            (g + number + 1) % 2,
            number > 1,
            number < PASSES,
            number in (1, 3),
            number == PASSES,
        )

    def drain(t, carry):
        for b in (0, 1):
            each_side(lambda q, b=b: v_copy(b, t, q).wait_send())
        return carry

    lax.fori_loop(0, T, drain, 0)
    for item in range(3):
        each_side(lambda q, item=item: start_copy(item, q).wait_send())
    each_side(lambda q: hx_copy(q).wait_send())
    for d in range(1, H + 1):
        each_side(lambda q, d=d: cm_copy(q, d, False).wait_send(), d)
    for j in range(n_tm):
        for d in distances(j):
            each_side(lambda q, d=d, j=j: d_copy(j, q, d, False).wait_send(), d)
    for d in range(1, n_tm):
        r_copy(d).wait_send()

    @pl.when(k < n_tm - 1)
    def _():
        o_copy.wait_send()


def solution(mesh):
    n_tm, n_space = mesh.shape["tm"], mesh.shape["space"]

    def on_device(source, initial, mobility, labels, electrode, rates):
        T, X, Y, Z = source.shape
        A, YC = X // 2, Y // 2
        H = -(-n_tm // A)
        CP = A + 2 * A * H
        YP, CYP = Y + 2 * PAD, YC + 2 * PAD
        f32 = jnp.float32
        vm = pltpu.VMEM
        dma = pltpu.SemaphoreType.DMA
        in_vmem = pl.BlockSpec(memory_space=pltpu.VMEM)
        return pl.pallas_call(
            functools.partial(kernel, n_tm, n_space, rates.shape[0]),
            out_shape=jax.ShapeDtypeStruct(source.shape, f32),
            in_specs=[in_vmem] * 5 + [pl.BlockSpec(memory_space=pltpu.SMEM)],
            out_specs=in_vmem,
            scratch_shapes=[
                vm((2, T + 1, X + 2, YP, Z), f32),
                vm((X + 2, YP, Z), f32),
                vm((X + 2, YP, Z), f32),
                vm((2, Y, Z), jnp.int32),
                vm((T, X, Y, Z), f32),
                vm((X, Y, Z), f32),
                vm((X, Y, Z), f32),
                vm((X + 2, Y, Z), f32),
                vm((X, Y, Z), f32),
                vm((X + 1, Y, Z), f32),
                vm((X, YP, Z), f32),
                vm((X, Y, Z), f32),
                vm((X, Y, Z), f32),
                vm((X, Y, Z), f32),
                vm((X + 2, YP, Z), f32),
                vm((max(A, 2), Y, Z), f32),
                vm((2, YC, Z), f32),
                vm((2, YC, Z), f32),
                vm((A, YC, Z), f32),
                vm((A, YC, Z), f32),
                vm((X, Y, Z), f32),
                vm((CP, CYP, Z), f32),
                vm((CP + 1, YC, Z), f32),
                vm((CP, CYP, Z), f32),
                vm((CP, YC, Z), f32),
                vm((CP, YC, Z), f32),
                vm((CP, YC, Z), f32),
                vm((n_tm, CP, YC, Z), f32),
                vm((n_tm, CP, CYP, Z), f32),
                vm((X + 2, Y, Z), f32),
                dma((3, 2)),
                dma((3, 2)),
                dma((2, 2, T)),
                dma((2, 2, T)),
                dma((2 * H,)),
                dma((2 * H,)),
                dma((2,)),
                dma((2,)),
                dma,
                dma,
                dma((n_tm,)),
                dma((n_tm,)),
                dma((n_tm, 2 * H)),
                dma((n_tm, 2 * H)),
                dma,
                dma,
            ],
            compiler_params=pltpu.CompilerParams(
                collective_id=0, has_side_effects=True, vmem_limit_bytes=60 * 2**20
            ),
        )(source, initial, mobility, labels, electrode, rates)

    return jax.shard_map(
        on_device,
        mesh=mesh,
        in_specs=(
            P("tm", "space", None, None),
            P("space", None, None),
            P("space", None, None),
            P("space", None, None),
            P("space", None, None),
            P(),
        ),
        out_specs=P("tm", "space", None, None),
        check_vma=False,
    )
```

```python
import functools

import jax
import jax.numpy as jnp
from jax import lax
from jax.experimental import pallas as pl
from jax.experimental.pallas import tpu as pltpu
from jax.sharding import PartitionSpec as P

PASSES = 4

source_coef = 0.5
drift_coef = 0.5
react_coef = 0.5
damping = 0.8
coarse_lateral = 0.06
coarse_axial = 0.12

PAD = 8
CHUNK = 16


def kernel(
    n_tm,
    n_space,
    regions,
    source,
    initial,
    mobility,
    labels,
    electrode,
    rates,
    out,
    V,
    IE,
    ME,
    EB,
    F,
    FS,
    KP,
    FR,
    FW,
    FX,
    FY,
    FZ,
    BZ,
    AZ,
    D0,
    W,
    TMP,
    HS,
    HX,
    OS,
    OB,
    VO,
    CM,
    GX,
    GY,
    GL,
    GH,
    GD,
    R,
    C,
    UP,
    s_init,
    r_init,
    s_v,
    r_v,
    s_cm,
    r_cm,
    s_hx,
    r_hx,
    s_o,
    r_o,
    s_r,
    r_r,
    s_d,
    r_d,
    s_vo,
    r_vo,
):
    T, X, Y, Z = source.shape
    A, YC = X // 2, Y // 2
    H = -(-n_tm // A)
    E = A * H
    CP = A + 2 * E
    rows = pl.ds(PAD, Y)
    crows = pl.ds(PAD, YC)
    k = lax.axis_index("tm")
    s = lax.axis_index("space")

    def beyond(q, d=1):
        return s >= d if q == 0 else s + d < n_space

    def space_id(q, d=1):
        return {"space": s - d if q == 0 else s + d}

    def remote(src, dst, send, recv, where):
        return pltpu.make_async_remote_copy(
            src_ref=src,
            dst_ref=dst,
            send_sem=send,
            recv_sem=recv,
            device_id=where,
            device_id_type=pl.DeviceIdType.MESH,
        )

    def each_side(action, d=1):
        for q in (0, 1):
            pl.when(beyond(q, d))(functools.partial(action, q))

    barrier = pltpu.get_barrier_semaphore()

    def greet(where):
        pl.semaphore_signal(
            barrier, inc=1, device_id=where, device_id_type=pl.DeviceIdType.MESH
        )

    for d in range(1, H + 1):
        each_side(lambda q, d=d: greet(space_id(q, d)), d)
    for d in range(1, n_tm):
        greet({"tm": lax.rem(k + d, n_tm)})

    edge = jnp.zeros((PAD, Z), jnp.float32)
    plane = jnp.zeros((Y, Z), jnp.float32)
    cplane = jnp.zeros((YC, Z), jnp.float32)
    top, bottom = pl.ds(0, PAD), pl.ds(PAD + Y, PAD)
    ctop, cbottom = pl.ds(0, PAD), pl.ds(PAD + YC, PAD)
    for x in range(X + 2):
        for ref in (IE, ME, W):
            ref[x, top] = edge
            ref[x, bottom] = edge

        def clear(i, carry, x=x):
            for b in (0, 1):
                V[b, i, x, top] = edge
                V[b, i, x, bottom] = edge
            return carry

        lax.fori_loop(1, T + 1, clear, 0)
    for x in range(X):
        FY[x, bottom] = edge
        IE[x + 1, rows] = initial[x]
        ME[x + 1, rows] = mobility[x]
        for b in (0, 1):
            V[b, 0, x + 1, rows] = initial[x]
    W[0, rows] = plane
    W[X + 1, rows] = plane

    def clear_coarse(p, carry):
        for ref in (CM, GY):
            ref[p, ctop] = edge
            ref[p, cbottom] = edge
        for j in range(n_tm):
            C[j, p, ctop] = edge
            C[j, p, cbottom] = edge
        return carry

    lax.fori_loop(0, CP, clear_coarse, 0)
    for q in (0, 1):

        @pl.when(jnp.logical_not(beyond(q)))
        def _(q=q):
            x = 0 if q == 0 else X + 1
            IE[x, rows] = plane
            ME[x, rows] = plane
            FR[x] = plane
            HX[q] = cplane

            def clear_halo(i, carry):
                for b in (0, 1):
                    V[b, i, x, rows] = plane
                return carry

            lax.fori_loop(1, T + 1, clear_halo, 0)

        for d in range(1, H + 1):

            @pl.when(jnp.logical_not(beyond(q, d)))
            def _(q=q, d=d):
                for a in range(A):
                    p = E - A * d + a if q == 0 else E + A * d + a
                    CM[p, crows] = cplane
                    for j in range(n_tm):
                        R[j, p] = cplane

    peers = jnp.minimum(s, H) + jnp.minimum(n_space - 1 - s, H) + (n_tm - 1)
    pl.semaphore_wait(barrier, peers)

    def start_copy(item, q):
        src, dst = ((initial, IE), (mobility, ME), (electrode, EB))[item]
        x = 0 if q == 0 else X - 1
        if item < 2:
            target = dst.at[X + 1 if q == 0 else 0, rows]
        else:
            target = dst.at[1 - q]
        return remote(src.at[x], target, s_init.at[item, q], r_init.at[item, 1 - q], space_id(q))

    def landed(item, q):
        src, dst = ((initial, IE), (mobility, ME), (electrode, EB))[item]
        if item < 2:
            target = dst.at[0 if q == 0 else X + 1, rows]
        else:
            target = dst.at[q]
        return remote(src.at[0], target, s_init.at[item, q], r_init.at[item, q], space_id(q))

    for item in (1, 0, 2):
        each_side(lambda q, item=item: start_copy(item, q).start())

    def pair_rows(value, slot):
        TMP[slot] = value
        return TMP[slot, pl.ds(0, YC, stride=2), :] + TMP[slot, pl.ds(1, YC, stride=2), :]

    for a in range(A):
        CM[E + a, crows] = 0.25 * pair_rows(mobility[2 * a] + mobility[2 * a + 1], a)

    def reach(j, d):
        return min(A, n_tm - j - A * (d - 1))

    def deep(ref, pick, j, q, d, send, recv, incoming):
        n = reach(j, d)
        mine = E if q == 0 else E + A - n
        if incoming:
            there = E - A * d + A - n if q == 0 else E + A * d
        else:
            there = E + A * d if q == 0 else E - A * d + A - n
        slot = 2 * (d - 1)
        return remote(
            pick(ref, mine, n),
            pick(ref, there, n),
            send(slot + q),
            recv(slot + (q if incoming else 1 - q)),
            space_id(q, d),
        )

    def cm_copy(q, d, incoming):
        return deep(
            CM,
            lambda ref, p, n: ref.at[pl.ds(p, n), crows],
            0,
            q,
            d,
            lambda i: s_cm.at[i],
            lambda i: r_cm.at[i],
            incoming,
        )

    for d in range(1, H + 1):
        each_side(lambda q, d=d: cm_copy(q, d, False).start(), d)

    lane = lax.broadcasted_iota(jnp.int32, (Y, Z), 1)
    not_first, not_last = lane > 0, lane < Z - 1

    def half_forcing(t, carry):
        for x in range(X):
            F[t, x] = source_coef * source[t, x]
        return carry

    lax.fori_loop(0, T, half_forcing, 0)
    for x in range(X):
        total = F[0, x]
        for t in range(1, T):
            total = total + F[t, x]
        FS[x] = total
        lab = labels[x]
        rate = jnp.zeros((Y, Z), jnp.float32)
        for i in range(regions):
            rate = jnp.where(lab == i, rates[i], rate)
        KP[x] = react_coef * rate
        free = 1.0 - electrode[x].astype(jnp.float32)
        FR[x + 1] = free
        FW[x] = damping * free
        mid = mobility[x]
        FY[x, rows] = 0.5 * (mid + ME[x + 1, pl.ds(PAD - 1, Y)])
        FY[x, pl.ds(PAD + Y, 1)] = 0.5 * mobility[x, pl.ds(Y - 1, 1)]
        low = 0.5 * (mid + jnp.where(not_first, pltpu.roll(mid, 1, 1), 0.0))
        high = 0.5 * (mid + jnp.where(not_last, pltpu.roll(mid, Z - 1, 1), 0.0))
        BZ[x] = jnp.where(not_first, (1.0 + drift_coef) * low, 0.0)
        AZ[x] = jnp.where(not_last, high, 0.0)
        FZ[x] = FY[x, pl.ds(PAD + 1, Y)]
        D0[x] = 1.0 + low + (1.0 + drift_coef) * high + FY[x, rows] + FY[x, pl.ds(PAD + 1, Y)]
    for x in range(1, X):
        FX[x] = 0.5 * (mobility[x - 1] + mobility[x])

    @pl.when(k == 0)
    def _():
        for a in range(A):
            OB[a] = pair_rows(initial[2 * a] + initial[2 * a + 1], a)

    each_side(lambda q: landed(1, q).wait_recv())
    FX[0] = 0.5 * (ME[0, rows] + ME[1, rows])
    FX[X] = 0.5 * (ME[X, rows] + ME[X + 1, rows])
    for x in range(X):
        D0[x] = D0[x] + FX[x] + FX[x + 1]

    def around(read, x, centre, r=0, n=Y):
        i = x - 1
        here = pl.ds(r, n)
        return (
            FX[i, here] * read(x - 1, PAD + r)
            + FX[i + 1, here] * read(x + 1, PAD + r)
            + FY[i, pl.ds(PAD + r, n)] * read(x, PAD + r - 1)
            + FZ[i, here] * read(x, PAD + r + 1)
            + BZ[i, here] * pltpu.roll(centre, 1, 1)
            + AZ[i, here] * pltpu.roll(centre, Z - 1, 1)
        )

    def v_copy(b, t, q):
        x = 1 if q == 0 else X
        there = X + 1 if q == 0 else 0
        return remote(
            V.at[b, t + 1, x, rows],
            V.at[b, t + 1, there, rows],
            s_v.at[b, q, t],
            r_v.at[b, 1 - q, t],
            space_id(q),
        )

    def v_landed(b, t, q):
        x = 0 if q == 0 else X + 1
        return remote(
            V.at[b, t + 1, 1, rows],
            V.at[b, t + 1, x, rows],
            s_v.at[b, q, t],
            r_v.at[b, q, t],
            space_id(q),
        )

    each_side(lambda q: landed(0, q).wait_recv())

    def first_plane(x):
        i = x - 1
        now = IE[x, rows]
        half = KP[i] * jnp.abs(now)
        part = D0[i] + half
        common = around(lambda xx, o: IE[xx, pl.ds(o, Y)], x, now) + now - now * part
        TMP[0] = common
        TMP[1] = FW[i] / (part + half)

        def step(t, carry):
            V[1, t + 1, x, rows] = IE[x, rows] + TMP[1] * (F[t, i] + TMP[0])
            if x in (1, X):
                q = 0 if x == 1 else 1
                pl.when(beyond(q))(lambda: v_copy(1, t, q).start())
            return carry

        lax.fori_loop(0, T, step, 0)

    for x in (1, X) + tuple(range(2, X)):
        first_plane(x)

    def relaxed(b, t, x, r, n):
        i = x - 1
        here, mine = pl.ds(r, n), pl.ds(PAD + r, n)
        now = V[b, t + 1, x, mine]
        half = KP[i, here] * jnp.abs(now)
        part = D0[i, here] + half
        gain = (
            around(lambda xx, o: V[b, t + 1, xx, pl.ds(o, n)], x, now, r, n)
            + (F[t, i, here] + V[b, t, x, mine])
            - now * part
        )
        return now + FW[i, here] * gain / (part + half)

    def one_pass(b, arriving, sending, free_send, last):
        o = 1 - b

        def store(t, x):
            for r in range(0, Y, CHUNK):
                value = relaxed(b, t, x, r, CHUNK)
                if last:
                    out[t, x - 1, pl.ds(r, CHUNK)] = value
                else:
                    V[o, t + 1, x, pl.ds(PAD + r, CHUNK)] = value

        def step(t, carry):
            if arriving:
                each_side(lambda q: v_landed(b, t, q).wait_recv())
            if free_send:
                each_side(lambda q: v_copy(o, t, q).wait_send())
            for q, x in ((0, 1), (1, X)):
                store(t, x)
            if sending:
                each_side(lambda q: v_copy(o, t, q).start())
            for x in range(2, X):
                store(t, x)
            return carry

        lax.fori_loop(0, T, step, 0)

    for number in range(2, PASSES + 1):
        one_pass((number + 1) % 2, True, number < PASSES, number > 2, False)
    g = PASSES % 2

    def total_of(x):
        total = V[g, 1, x, rows]
        for t in range(1, T):
            total = total + V[g, t + 1, x, rows]
        return total

    def hx_copy(q):
        return remote(HS.at[q], HX.at[1 - q], s_hx.at[q], r_hx.at[1 - q], space_id(q))

    def hx_landed(q):
        return remote(HS.at[q], HX.at[q], s_hx.at[q], r_hx.at[q], space_id(q))

    for q, x in ((0, 1), (1, X)):
        total = total_of(x)
        W[x, rows] = total
        HS[q] = 0.25 * pair_rows(FX[0 if q == 0 else X] * total, q)
        pl.when(beyond(q))(functools.partial(lambda q: hx_copy(q).start(), q))

    o_copy = remote(OS, OB, s_o, r_o, {"tm": lax.rem(k + 1, n_tm)})
    for a in range(A):
        OS[a] = pair_rows(V[g, T, 2 * a + 1, rows] + V[g, T, 2 * a + 2, rows], a)

    @pl.when(k < n_tm - 1)
    def _():
        o_copy.start()

    def v_out(t, carry):
        each_side(lambda q: v_copy(g, t, q).start())
        return carry

    lax.fori_loop(0, T, v_out, 0)

    for x in range(2, X):
        W[x, rows] = total_of(x)

    def residual_sum(x):
        i = x - 1
        total = W[x, rows]
        quad = jnp.zeros((Y, Z), jnp.float32)
        for t in range(T):
            value = V[g, t + 1, x, rows]
            quad = quad + value * jnp.abs(value)
        return (
            FS[i]
            + (total - V[g, T, x, rows])
            + around(lambda xx, o: W[xx, pl.ds(o, Y)], x, total)
            - D0[i] * total
            - KP[i] * quad
        )

    own = []
    for a in range(A):
        own.append(pair_rows(residual_sum(2 * a + 1) + residual_sum(2 * a + 2), a))

    @pl.when(k > 0)
    def _():
        o_copy.wait_recv()

    each_side(lambda q: hx_landed(q).wait_recv())
    for a in range(A):
        value = 0.25 * (own[a] + OB[a])
        if a == 0:
            value = value + HX[0]
        if a == A - 1:
            value = value + HX[1]
        R[k, E + a] = value

    def r_copy(d):
        return remote(
            R.at[k, pl.ds(E, A)],
            R.at[k, pl.ds(E, A)],
            s_r.at[d],
            r_r.at[k],
            {"tm": lax.rem(k + d, n_tm)},
        )

    def r_landed(j):
        return remote(
            R.at[j, pl.ds(E, A)],
            R.at[j, pl.ds(E, A)],
            s_r.at[0],
            r_r.at[j],
            {"tm": lax.rem(k + 1, n_tm)},
        )

    for d in range(n_tm - 1, 0, -1):
        r_copy(d).start()

    vo_copy = remote(
        V.at[g, T, pl.ds(1, X), rows], VO, s_vo, r_vo, {"tm": lax.rem(k + 1, n_tm)}
    )

    @pl.when(k < n_tm - 1)
    def _():
        vo_copy.start()

    for d in range(1, H + 1):
        each_side(lambda q, d=d: cm_copy(q, d, True).wait_recv(), d)
    clane = lax.broadcasted_iota(jnp.int32, (YC, Z), 1)
    c_first, c_last = clane > 0, clane < Z - 1
    lo = E - (n_tm - 1)
    hi = E + A + (n_tm - 1)

    def coarse_faces(p, carry):
        GX[p] = (0.5 * coarse_lateral) * (CM[p - 1, crows] + CM[p, crows])
        return carry

    lax.fori_loop(lo, hi + 1, coarse_faces, 0)

    def coarse_coefs(p, carry):
        mid = CM[p, crows]
        near = (0.5 * coarse_lateral) * (mid + CM[p, pl.ds(PAD - 1, YC)])
        far = (0.5 * coarse_lateral) * (mid + CM[p, pl.ds(PAD + 1, YC)])
        GY[p, crows] = near
        low = (0.5 * coarse_axial) * (
            mid + jnp.where(c_first, pltpu.roll(mid, 1, 1), 0.0)
        )
        high = (0.5 * coarse_axial) * (
            mid + jnp.where(c_last, pltpu.roll(mid, Z - 1, 1), 0.0)
        )
        GL[p] = jnp.where(c_first, low, 0.0)
        GH[p] = jnp.where(c_last, high, 0.0)
        GD[p] = 1.0 - (GX[p] + GX[p + 1] + near + far + low + high)
        return carry

    lax.fori_loop(lo, hi, coarse_coefs, 0)

    def d_copy(j, q, d, incoming):
        return deep(
            R,
            lambda ref, p, n: ref.at[j, pl.ds(p, n)],
            j,
            q,
            d,
            lambda i: s_d.at[j, i],
            lambda i: r_d.at[j, i],
            incoming,
        )

    def distances(j):
        return [d for d in range(1, H + 1) if reach(j, d) > 0]

    for j in range(n_tm):
        pl.when(k != j)(lambda j=j: r_landed(j).wait_recv())
        for d in distances(j):
            each_side(lambda q, d=d, j=j: d_copy(j, q, d, False).start(), d)

    for j in range(n_tm):
        for d in distances(j):
            each_side(lambda q, d=d, j=j: d_copy(j, q, d, True).wait_recv(), d)

        def coarse_plane(p, carry, j=j):
            if j == 0:
                C[0, p, crows] = R[0, p]
                return carry
            mid = C[j - 1, p, crows]
            value = (
                R[j, p]
                + GD[p] * mid
                + GX[p] * C[j - 1, p - 1, crows]
                + GX[p + 1] * C[j - 1, p + 1, crows]
                + GY[p, crows] * C[j - 1, p, pl.ds(PAD - 1, YC)]
                + GY[p, pl.ds(PAD + 1, YC)] * C[j - 1, p, pl.ds(PAD + 1, YC)]
                + GL[p] * pltpu.roll(mid, 1, 1)
                + GH[p] * pltpu.roll(mid, Z - 1, 1)
            )
            where = A * s + p - E
            inside = jnp.logical_and(where >= 0, where < A * n_space)
            C[j, p, crows] = jnp.where(inside, value, 0.0)
            return carry

        width = n_tm - j
        lax.fori_loop(E - width, E + A + width, coarse_plane, 0, unroll=2)

    each_side(lambda q: landed(2, q).wait_recv())
    for q in (0, 1):

        @pl.when(beyond(q))
        def _(q=q):
            FR[0 if q == 0 else X + 1] = 1.0 - EB[q].astype(jnp.float32)

    def spread(j, x):
        value = C[j, E + (x + 1) // 2 - 1, crows]
        UP[x, pl.ds(0, YC, stride=2), :] = value
        UP[x, pl.ds(1, YC, stride=2), :] = value
        return FR[x] * UP[x]

    def v_home(t, carry):
        each_side(lambda q: v_copy(g, t, q).wait_send())
        each_side(lambda q: v_landed(g, t, q).wait_recv())
        return carry

    lax.fori_loop(0, T, v_home, 0)

    @pl.when(k < n_tm - 1)
    def _():
        vo_copy.wait_send()

    for x in range(X + 2):
        move = spread(k, x)
        for t in range(T):
            V[g, t + 1, x, rows] = V[g, t + 1, x, rows] + move

    @pl.when(k > 0)
    def _():
        vo_copy.wait_recv()
        for x in range(1, X + 1):
            opening = VO[x - 1] + spread(k - 1, x)
            for b in (0, 1):
                V[b, 0, x, rows] = opening

    for number in range(1, PASSES + 1):
        one_pass(
            (g + number + 1) % 2,
            number > 1,
            number < PASSES,
            number in (1, 3),
            number == PASSES,
        )

    def drain(t, carry):
        for b in (0, 1):
            each_side(lambda q, b=b: v_copy(b, t, q).wait_send())
        return carry

    lax.fori_loop(0, T, drain, 0)
    for item in range(3):
        each_side(lambda q, item=item: start_copy(item, q).wait_send())
    each_side(lambda q: hx_copy(q).wait_send())
    for d in range(1, H + 1):
        each_side(lambda q, d=d: cm_copy(q, d, False).wait_send(), d)
    for j in range(n_tm):
        for d in distances(j):
            each_side(lambda q, d=d, j=j: d_copy(j, q, d, False).wait_send(), d)
    for d in range(1, n_tm):
        r_copy(d).wait_send()

    @pl.when(k < n_tm - 1)
    def _():
        o_copy.wait_send()


def solution(mesh):
    n_tm, n_space = mesh.shape["tm"], mesh.shape["space"]

    def on_device(source, initial, mobility, labels, electrode, rates):
        T, X, Y, Z = source.shape
        A, YC = X // 2, Y // 2
        H = -(-n_tm // A)
        CP = A + 2 * A * H
        YP, CYP = Y + 2 * PAD, YC + 2 * PAD
        f32 = jnp.float32
        vm = pltpu.VMEM
        dma = pltpu.SemaphoreType.DMA
        in_vmem = pl.BlockSpec(memory_space=pltpu.VMEM)
        return pl.pallas_call(
            functools.partial(kernel, n_tm, n_space, rates.shape[0]),
            out_shape=jax.ShapeDtypeStruct(source.shape, f32),
            in_specs=[in_vmem] * 5 + [pl.BlockSpec(memory_space=pltpu.SMEM)],
            out_specs=in_vmem,
            scratch_shapes=[
                vm((2, T + 1, X + 2, YP, Z), f32),
                vm((X + 2, YP, Z), f32),
                vm((X + 2, YP, Z), f32),
                vm((2, Y, Z), jnp.int32),
                vm((T, X, Y, Z), f32),
                vm((X, Y, Z), f32),
                vm((X, Y, Z), f32),
                vm((X + 2, Y, Z), f32),
                vm((X, Y, Z), f32),
                vm((X + 1, Y, Z), f32),
                vm((X, YP, Z), f32),
                vm((X, Y, Z), f32),
                vm((X, Y, Z), f32),
                vm((X, Y, Z), f32),
                vm((X, Y, Z), f32),
                vm((X + 2, YP, Z), f32),
                vm((max(A, 2), Y, Z), f32),
                vm((2, YC, Z), f32),
                vm((2, YC, Z), f32),
                vm((A, YC, Z), f32),
                vm((A, YC, Z), f32),
                vm((X, Y, Z), f32),
                vm((CP, CYP, Z), f32),
                vm((CP + 1, YC, Z), f32),
                vm((CP, CYP, Z), f32),
                vm((CP, YC, Z), f32),
                vm((CP, YC, Z), f32),
                vm((CP, YC, Z), f32),
                vm((n_tm, CP, YC, Z), f32),
                vm((n_tm, CP, CYP, Z), f32),
                vm((X + 2, Y, Z), f32),
                dma((3, 2)),
                dma((3, 2)),
                dma((2, 2, T)),
                dma((2, 2, T)),
                dma((2 * H,)),
                dma((2 * H,)),
                dma((2,)),
                dma((2,)),
                dma,
                dma,
                dma((n_tm,)),
                dma((n_tm,)),
                dma((n_tm, 2 * H)),
                dma((n_tm, 2 * H)),
                dma,
                dma,
            ],
            compiler_params=pltpu.CompilerParams(
                collective_id=0, has_side_effects=True, vmem_limit_bytes=60 * 2**20
            ),
        )(source, initial, mobility, labels, electrode, rates)

    return jax.shard_map(
        on_device,
        mesh=mesh,
        in_specs=(
            P("tm", "space", None, None),
            P("space", None, None),
            P("space", None, None),
            P("space", None, None),
            P("space", None, None),
            P(),
        ),
        out_specs=P("tm", "space", None, None),
        check_vma=False,
    )
```

```python
import functools

import jax
import jax.numpy as jnp
from jax import lax
from jax.experimental import pallas as pl
from jax.experimental.pallas import tpu as pltpu
from jax.sharding import PartitionSpec as P

PASSES = 4

source_coef = 0.5
drift_coef = 0.5
react_coef = 0.5
damping = 0.8
coarse_lateral = 0.06
coarse_axial = 0.12

PAD = 8
CHUNK = 16


def kernel(
    n_tm,
    n_space,
    regions,
    source_far,
    initial_far,
    mobility_far,
    labels_far,
    electrode_far,
    rates,
    out_far,
    source,
    initial,
    mobility,
    labels,
    electrode,
    out,
    s_in,
    s_out,
    V,
    IE,
    ME,
    EB,
    F,
    FS,
    KP,
    FR,
    FW,
    FX,
    FY,
    FZ,
    BZ,
    AZ,
    D0,
    W,
    TMP,
    HS,
    HX,
    OS,
    OB,
    VO,
    VS,
    CM,
    GX,
    GY,
    GL,
    GH,
    GD,
    R,
    C,
    UP,
    s_init,
    r_init,
    s_v,
    r_v,
    s_cm,
    r_cm,
    s_hx,
    r_hx,
    s_o,
    r_o,
    s_r,
    r_r,
    s_d,
    r_d,
    s_vo,
    r_vo,
):
    T, X, Y, Z = source.shape
    A, YC = X // 2, Y // 2
    H = -(-n_tm // A)
    E = A * H
    CP = A + 2 * E
    rows = pl.ds(PAD, Y)
    crows = pl.ds(PAD, YC)
    k = lax.axis_index("tm")
    s = lax.axis_index("space")

    def beyond(q, d=1):
        return s >= d if q == 0 else s + d < n_space

    def space_id(q, d=1):
        return {"space": s - d if q == 0 else s + d}

    def remote(src, dst, send, recv, where):
        return pltpu.make_async_remote_copy(
            src_ref=src,
            dst_ref=dst,
            send_sem=send,
            recv_sem=recv,
            device_id=where,
            device_id_type=pl.DeviceIdType.MESH,
        )

    def each_side(action, d=1):
        for q in (0, 1):
            pl.when(beyond(q, d))(functools.partial(action, q))

    barrier = pltpu.get_barrier_semaphore()

    def greet(where):
        pl.semaphore_signal(
            barrier, inc=1, device_id=where, device_id_type=pl.DeviceIdType.MESH
        )

    for d in range(1, H + 1):
        each_side(lambda q, d=d: greet(space_id(q, d)), d)
    for d in range(1, n_tm):
        greet({"tm": lax.rem(k + d, n_tm)})

    fetches = [
        pltpu.make_async_copy(far, near, s_in.at[i])
        for i, (far, near) in enumerate(
            (
                (mobility_far, mobility),
                (initial_far, initial),
                (electrode_far, electrode),
                (labels_far, labels),
                (source_far, source),
            )
        )
    ]
    for fetch in fetches:
        fetch.start()

    edge = jnp.zeros((PAD, Z), jnp.float32)
    plane = jnp.zeros((Y, Z), jnp.float32)
    cplane = jnp.zeros((YC, Z), jnp.float32)
    top, bottom = pl.ds(0, PAD), pl.ds(PAD + Y, PAD)
    ctop, cbottom = pl.ds(0, PAD), pl.ds(PAD + YC, PAD)
    for x in range(X + 2):
        for ref in (IE, ME, W):
            ref[x, top] = edge
            ref[x, bottom] = edge

        def clear(i, carry, x=x):
            for b in (0, 1):
                V[b, i, x, top] = edge
                V[b, i, x, bottom] = edge
            return carry

        lax.fori_loop(1, T + 1, clear, 0)
    for x in range(X):
        FY[x, bottom] = edge
    W[0, rows] = plane
    W[X + 1, rows] = plane

    def clear_coarse(p, carry):
        for ref in (CM, GY):
            ref[p, ctop] = edge
            ref[p, cbottom] = edge
        for j in range(n_tm):
            C[j, p, ctop] = edge
            C[j, p, cbottom] = edge
        return carry

    lax.fori_loop(0, CP, clear_coarse, 0)
    for q in (0, 1):

        @pl.when(jnp.logical_not(beyond(q)))
        def _(q=q):
            x = 0 if q == 0 else X + 1
            IE[x, rows] = plane
            ME[x, rows] = plane
            FR[x] = plane
            HX[q] = cplane

            def clear_halo(i, carry):
                for b in (0, 1):
                    V[b, i, x, rows] = plane
                return carry

            lax.fori_loop(1, T + 1, clear_halo, 0)

        for d in range(1, H + 1):

            @pl.when(jnp.logical_not(beyond(q, d)))
            def _(q=q, d=d):
                for a in range(A):
                    p = E - A * d + a if q == 0 else E + A * d + a
                    CM[p, crows] = cplane
                    for j in range(n_tm):
                        R[j, p] = cplane

    peers = jnp.minimum(s, H) + jnp.minimum(n_space - 1 - s, H) + (n_tm - 1)
    pl.semaphore_wait(barrier, peers)

    def start_copy(item, q):
        src, dst = ((initial_far, IE), (mobility_far, ME), (electrode_far, EB))[item]
        x = 0 if q == 0 else X - 1
        if item < 2:
            target = dst.at[X + 1 if q == 0 else 0, rows]
        else:
            target = dst.at[1 - q]
        return remote(src.at[x], target, s_init.at[item, q], r_init.at[item, 1 - q], space_id(q))

    def landed(item, q):
        src, dst = ((initial_far, IE), (mobility_far, ME), (electrode_far, EB))[item]
        if item < 2:
            target = dst.at[0 if q == 0 else X + 1, rows]
        else:
            target = dst.at[q]
        return remote(src.at[0], target, s_init.at[item, q], r_init.at[item, q], space_id(q))

    for item in (1, 0, 2):
        each_side(lambda q, item=item: start_copy(item, q).start())

    for fetch in fetches[:2]:
        fetch.wait()
    for x in range(X):
        IE[x + 1, rows] = initial[x]
        ME[x + 1, rows] = mobility[x]
        for b in (0, 1):
            V[b, 0, x + 1, rows] = initial[x]

    def pair_rows(value, slot):
        TMP[slot] = value
        return TMP[slot, pl.ds(0, YC, stride=2), :] + TMP[slot, pl.ds(1, YC, stride=2), :]

    for a in range(A):
        CM[E + a, crows] = 0.25 * pair_rows(mobility[2 * a] + mobility[2 * a + 1], a)

    def reach(j, d):
        return min(A, n_tm - j - A * (d - 1))

    def deep(ref, pick, j, q, d, send, recv, incoming):
        n = reach(j, d)
        mine = E if q == 0 else E + A - n
        if incoming:
            there = E - A * d + A - n if q == 0 else E + A * d
        else:
            there = E + A * d if q == 0 else E - A * d + A - n
        slot = 2 * (d - 1)
        return remote(
            pick(ref, mine, n),
            pick(ref, there, n),
            send(slot + q),
            recv(slot + (q if incoming else 1 - q)),
            space_id(q, d),
        )

    def cm_copy(q, d, incoming):
        return deep(
            CM,
            lambda ref, p, n: ref.at[pl.ds(p, n), crows],
            0,
            q,
            d,
            lambda i: s_cm.at[i],
            lambda i: r_cm.at[i],
            incoming,
        )

    for d in range(1, H + 1):
        each_side(lambda q, d=d: cm_copy(q, d, False).start(), d)

    for fetch in fetches[2:]:
        fetch.wait()
    lane = lax.broadcasted_iota(jnp.int32, (Y, Z), 1)
    not_first, not_last = lane > 0, lane < Z - 1

    def half_forcing(t, carry):
        for x in range(X):
            F[t, x] = source_coef * source[t, x]
        return carry

    lax.fori_loop(0, T, half_forcing, 0)
    for x in range(X):
        total = F[0, x]
        for t in range(1, T):
            total = total + F[t, x]
        FS[x] = total
        lab = labels[x]
        rate = jnp.zeros((Y, Z), jnp.float32)
        for i in range(regions):
            rate = jnp.where(lab == i, rates[i], rate)
        KP[x] = react_coef * rate
        free = 1.0 - electrode[x].astype(jnp.float32)
        FR[x + 1] = free
        FW[x] = damping * free
        mid = mobility[x]
        FY[x, rows] = 0.5 * (mid + ME[x + 1, pl.ds(PAD - 1, Y)])
        FY[x, pl.ds(PAD + Y, 1)] = 0.5 * mobility[x, pl.ds(Y - 1, 1)]
        low = 0.5 * (mid + jnp.where(not_first, pltpu.roll(mid, 1, 1), 0.0))
        high = 0.5 * (mid + jnp.where(not_last, pltpu.roll(mid, Z - 1, 1), 0.0))
        BZ[x] = jnp.where(not_first, (1.0 + drift_coef) * low, 0.0)
        AZ[x] = jnp.where(not_last, high, 0.0)
        FZ[x] = FY[x, pl.ds(PAD + 1, Y)]
        D0[x] = 1.0 + low + (1.0 + drift_coef) * high + FY[x, rows] + FY[x, pl.ds(PAD + 1, Y)]
    for x in range(1, X):
        FX[x] = 0.5 * (mobility[x - 1] + mobility[x])

    @pl.when(k == 0)
    def _():
        for a in range(A):
            OB[a] = pair_rows(initial[2 * a] + initial[2 * a + 1], a)

    each_side(lambda q: landed(1, q).wait_recv())
    FX[0] = 0.5 * (ME[0, rows] + ME[1, rows])
    FX[X] = 0.5 * (ME[X, rows] + ME[X + 1, rows])
    for x in range(X):
        D0[x] = D0[x] + FX[x] + FX[x + 1]

    def around(read, x, centre, r=0, n=Y):
        i = x - 1
        here = pl.ds(r, n)
        return (
            FX[i, here] * read(x - 1, PAD + r)
            + FX[i + 1, here] * read(x + 1, PAD + r)
            + FY[i, pl.ds(PAD + r, n)] * read(x, PAD + r - 1)
            + FZ[i, here] * read(x, PAD + r + 1)
            + BZ[i, here] * pltpu.roll(centre, 1, 1)
            + AZ[i, here] * pltpu.roll(centre, Z - 1, 1)
        )

    def v_copy(b, t, q):
        x = 1 if q == 0 else X
        there = X + 1 if q == 0 else 0
        return remote(
            V.at[b, t + 1, x, rows],
            V.at[b, t + 1, there, rows],
            s_v.at[b, q, t],
            r_v.at[b, 1 - q, t],
            space_id(q),
        )

    def v_landed(b, t, q):
        x = 0 if q == 0 else X + 1
        return remote(
            V.at[b, t + 1, 1, rows],
            V.at[b, t + 1, x, rows],
            s_v.at[b, q, t],
            r_v.at[b, q, t],
            space_id(q),
        )

    each_side(lambda q: landed(0, q).wait_recv())

    def first_plane(x):
        i = x - 1
        now = IE[x, rows]
        half = KP[i] * jnp.abs(now)
        part = D0[i] + half
        common = around(lambda xx, o: IE[xx, pl.ds(o, Y)], x, now) + now - now * part
        TMP[0] = common
        TMP[1] = FW[i] / (part + half)

        def step(index, carry):
            t = T - 1 - index
            V[1, t + 1, x, rows] = IE[x, rows] + TMP[1] * (F[t, i] + TMP[0])
            if x in (1, X):
                q = 0 if x == 1 else 1
                pl.when(beyond(q))(lambda: v_copy(1, t, q).start())
            return carry

        lax.fori_loop(0, T, step, 0)

    for x in (1, X) + tuple(range(2, X)):
        first_plane(x)

    def relaxed(b, t, x, r, n):
        i = x - 1
        here, mine = pl.ds(r, n), pl.ds(PAD + r, n)
        now = V[b, t + 1, x, mine]
        half = KP[i, here] * jnp.abs(now)
        part = D0[i, here] + half
        gain = (
            around(lambda xx, o: V[b, t + 1, xx, pl.ds(o, n)], x, now, r, n)
            + (F[t, i, here] + V[b, t, x, mine])
            - now * part
        )
        return now + FW[i, here] * gain / (part + half)

    def one_pass(
        b, arriving, sending, free_send, last, after_ends=None, after_last=None, before_first=None
    ):
        o = 1 - b

        def store(t, x):
            for r in range(0, Y, CHUNK):
                value = relaxed(b, t, x, r, CHUNK)
                if last:
                    out[t, x - 1, pl.ds(r, CHUNK)] = value
                else:
                    V[o, t + 1, x, pl.ds(PAD + r, CHUNK)] = value

        def leave(t):
            return pltpu.make_async_copy(out.at[t], out_far.at[t], s_out.at[t])

        def ends(index, carry):
            t = T - 1 - index
            if arriving:
                each_side(lambda q: v_landed(b, t, q).wait_recv())
            if free_send:
                each_side(lambda q: v_copy(o, t, q).wait_send())
            for q, x in ((0, 1), (1, X)):
                store(t, x)
            if sending:
                each_side(lambda q: v_copy(o, t, q).start())
            return carry

        def inner(index, carry):
            t = T - 1 - index
            for x in range(2, X):
                store(t, x)
            if last:
                leave(t).start()
            return carry

        def step(index, carry):
            return inner(index, ends(index, carry))

        if after_ends is not None:
            lax.fori_loop(0, T, ends, 0)
            after_ends()
            inner(0, 0)
            after_last()
            lax.fori_loop(1, T, inner, 0)
        elif before_first is not None:
            lax.fori_loop(0, T - 1, step, 0)
            before_first()
            lax.fori_loop(T - 1, T, step, 0)
        else:
            lax.fori_loop(0, T, step, 0)
        if last:
            for t in range(T):
                leave(t).wait()

    g = PASSES % 2

    def total_of(x):
        total = V[g, 1, x, rows]
        for t in range(1, T):
            total = total + V[g, t + 1, x, rows]
        return total

    def hx_copy(q):
        return remote(HS.at[q], HX.at[1 - q], s_hx.at[q], r_hx.at[1 - q], space_id(q))

    def hx_landed(q):
        return remote(HS.at[q], HX.at[q], s_hx.at[q], r_hx.at[q], space_id(q))

    def send_faces():
        for q, x in ((0, 1), (1, X)):
            total = total_of(x)
            W[x, rows] = total
            HS[q] = 0.25 * pair_rows(FX[0 if q == 0 else X] * total, q)
        each_side(lambda q: hx_copy(q).start())

        def v_out(index, carry):
            each_side(lambda q: v_copy(g, T - 1 - index, q).start())
            return carry

        lax.fori_loop(0, T, v_out, 0)

    o_copy = remote(OS, OB, s_o, r_o, {"tm": lax.rem(k + 1, n_tm)})
    vo_copy = remote(VS, VO, s_vo, r_vo, {"tm": lax.rem(k + 1, n_tm)})

    def send_last():
        for a in range(A):
            OS[a] = pair_rows(V[g, T, 2 * a + 1, rows] + V[g, T, 2 * a + 2, rows], a)
        for x in range(X):
            VS[x] = V[g, T, x + 1, rows]

        @pl.when(k < n_tm - 1)
        def _():
            o_copy.start()
            vo_copy.start()

    for number in range(2, PASSES):
        one_pass((number + 1) % 2, True, True, number > 2, False)
    one_pass((PASSES + 1) % 2, True, False, PASSES > 2, False, send_faces, send_last)

    for x in range(2, X):
        W[x, rows] = total_of(x)

    def residual_sum(x):
        i = x - 1
        total = W[x, rows]
        quad = jnp.zeros((Y, Z), jnp.float32)
        for t in range(T):
            value = V[g, t + 1, x, rows]
            quad = quad + value * jnp.abs(value)
        return (
            FS[i]
            + (total - V[g, T, x, rows])
            + around(lambda xx, o: W[xx, pl.ds(o, Y)], x, total)
            - D0[i] * total
            - KP[i] * quad
        )

    own = []
    for a in range(A):
        own.append(pair_rows(residual_sum(2 * a + 1) + residual_sum(2 * a + 2), a))

    @pl.when(k > 0)
    def _():
        o_copy.wait_recv()

    each_side(lambda q: hx_landed(q).wait_recv())
    for a in range(A):
        value = 0.25 * (own[a] + OB[a])
        if a == 0:
            value = value + HX[0]
        if a == A - 1:
            value = value + HX[1]
        R[k, E + a] = value

    def r_copy(d):
        return remote(
            R.at[k, pl.ds(E, A)],
            R.at[k, pl.ds(E, A)],
            s_r.at[d],
            r_r.at[k],
            {"tm": lax.rem(k + d, n_tm)},
        )

    def r_landed(j):
        return remote(
            R.at[j, pl.ds(E, A)],
            R.at[j, pl.ds(E, A)],
            s_r.at[0],
            r_r.at[j],
            {"tm": lax.rem(k + 1, n_tm)},
        )

    for d in range(n_tm - 1, 0, -1):
        r_copy(d).start()

    for d in range(1, H + 1):
        each_side(lambda q, d=d: cm_copy(q, d, True).wait_recv(), d)
    clane = lax.broadcasted_iota(jnp.int32, (YC, Z), 1)
    c_first, c_last = clane > 0, clane < Z - 1
    lo = E - (n_tm - 1)
    hi = E + A + (n_tm - 1)

    def coarse_faces(p, carry):
        GX[p] = (0.5 * coarse_lateral) * (CM[p - 1, crows] + CM[p, crows])
        return carry

    lax.fori_loop(lo, hi + 1, coarse_faces, 0)

    def coarse_coefs(p, carry):
        mid = CM[p, crows]
        near = (0.5 * coarse_lateral) * (mid + CM[p, pl.ds(PAD - 1, YC)])
        far = (0.5 * coarse_lateral) * (mid + CM[p, pl.ds(PAD + 1, YC)])
        GY[p, crows] = near
        low = (0.5 * coarse_axial) * (
            mid + jnp.where(c_first, pltpu.roll(mid, 1, 1), 0.0)
        )
        high = (0.5 * coarse_axial) * (
            mid + jnp.where(c_last, pltpu.roll(mid, Z - 1, 1), 0.0)
        )
        GL[p] = jnp.where(c_first, low, 0.0)
        GH[p] = jnp.where(c_last, high, 0.0)
        GD[p] = 1.0 - (GX[p] + GX[p + 1] + near + far + low + high)
        return carry

    lax.fori_loop(lo, hi, coarse_coefs, 0)

    def d_copy(j, q, d, incoming):
        return deep(
            R,
            lambda ref, p, n: ref.at[j, pl.ds(p, n)],
            j,
            q,
            d,
            lambda i: s_d.at[j, i],
            lambda i: r_d.at[j, i],
            incoming,
        )

    def distances(j):
        return [d for d in range(1, H + 1) if reach(j, d) > 0]

    for j in range(n_tm):
        pl.when(k != j)(lambda j=j: r_landed(j).wait_recv())
        for d in distances(j):
            each_side(lambda q, d=d, j=j: d_copy(j, q, d, False).start(), d)

    for j in range(n_tm):
        for d in distances(j):
            each_side(lambda q, d=d, j=j: d_copy(j, q, d, True).wait_recv(), d)

        def coarse_plane(p, carry, j=j):
            if j == 0:
                C[0, p, crows] = R[0, p]
                return carry
            mid = C[j - 1, p, crows]
            value = (
                R[j, p]
                + GD[p] * mid
                + GX[p] * C[j - 1, p - 1, crows]
                + GX[p + 1] * C[j - 1, p + 1, crows]
                + GY[p, crows] * C[j - 1, p, pl.ds(PAD - 1, YC)]
                + GY[p, pl.ds(PAD + 1, YC)] * C[j - 1, p, pl.ds(PAD + 1, YC)]
                + GL[p] * pltpu.roll(mid, 1, 1)
                + GH[p] * pltpu.roll(mid, Z - 1, 1)
            )
            where = A * s + p - E
            inside = jnp.logical_and(where >= 0, where < A * n_space)
            C[j, p, crows] = jnp.where(inside, value, 0.0)
            return carry

        width = n_tm - j
        lax.fori_loop(E - width, E + A + width, coarse_plane, 0, unroll=2)

    each_side(lambda q: landed(2, q).wait_recv())
    for q in (0, 1):

        @pl.when(beyond(q))
        def _(q=q):
            FR[0 if q == 0 else X + 1] = 1.0 - EB[q].astype(jnp.float32)

    def spread(j, x):
        value = C[j, E + (x + 1) // 2 - 1, crows]
        UP[x, pl.ds(0, YC, stride=2), :] = value
        UP[x, pl.ds(1, YC, stride=2), :] = value
        return FR[x] * UP[x]

    def v_home(t, carry):
        each_side(lambda q: v_copy(g, t, q).wait_send())
        each_side(lambda q: v_landed(g, t, q).wait_recv())
        return carry

    lax.fori_loop(0, T, v_home, 0)

    for x in range(X + 2):
        move = spread(k, x)
        for t in range(T):
            V[g, t + 1, x, rows] = V[g, t + 1, x, rows] + move

    def open_sweep():
        @pl.when(k > 0)
        def _():
            vo_copy.wait_recv()
            for x in range(1, X + 1):
                opening = VO[x - 1] + spread(k - 1, x)
                for b in (0, 1):
                    V[b, 0, x, rows] = opening

    for number in range(1, PASSES + 1):
        one_pass(
            (g + number + 1) % 2,
            number > 1,
            number < PASSES,
            number in (1, 3),
            number == PASSES,
            before_first=open_sweep if number == 1 else None,
        )

    def drain(t, carry):
        for b in (0, 1):
            each_side(lambda q, b=b: v_copy(b, t, q).wait_send())
        return carry

    lax.fori_loop(0, T, drain, 0)
    for item in range(3):
        each_side(lambda q, item=item: start_copy(item, q).wait_send())
    each_side(lambda q: hx_copy(q).wait_send())
    for d in range(1, H + 1):
        each_side(lambda q, d=d: cm_copy(q, d, False).wait_send(), d)
    for j in range(n_tm):
        for d in distances(j):
            each_side(lambda q, d=d, j=j: d_copy(j, q, d, False).wait_send(), d)
    for d in range(1, n_tm):
        r_copy(d).wait_send()

    @pl.when(k < n_tm - 1)
    def _():
        o_copy.wait_send()
        vo_copy.wait_send()


def solution(mesh):
    n_tm, n_space = mesh.shape["tm"], mesh.shape["space"]

    def on_device(source, initial, mobility, labels, electrode, rates):
        T, X, Y, Z = source.shape
        A, YC = X // 2, Y // 2
        H = -(-n_tm // A)
        CP = A + 2 * A * H
        YP, CYP = Y + 2 * PAD, YC + 2 * PAD
        f32 = jnp.float32
        vm = pltpu.VMEM
        dma = pltpu.SemaphoreType.DMA
        in_hbm = pl.BlockSpec(memory_space=pltpu.HBM)
        return pl.pallas_call(
            functools.partial(kernel, n_tm, n_space, rates.shape[0]),
            out_shape=jax.ShapeDtypeStruct(source.shape, f32),
            in_specs=[in_hbm] * 5 + [pl.BlockSpec(memory_space=pltpu.SMEM)],
            out_specs=in_hbm,
            scratch_shapes=[
                vm((T, X, Y, Z), f32),
                vm((X, Y, Z), f32),
                vm((X, Y, Z), f32),
                vm((X, Y, Z), jnp.int32),
                vm((X, Y, Z), jnp.int32),
                vm((T, X, Y, Z), f32),
                dma((5,)),
                dma((T,)),
                vm((2, T + 1, X + 2, YP, Z), f32),
                vm((X + 2, YP, Z), f32),
                vm((X + 2, YP, Z), f32),
                vm((2, Y, Z), jnp.int32),
                vm((T, X, Y, Z), f32),
                vm((X, Y, Z), f32),
                vm((X, Y, Z), f32),
                vm((X + 2, Y, Z), f32),
                vm((X, Y, Z), f32),
                vm((X + 1, Y, Z), f32),
                vm((X, YP, Z), f32),
                vm((X, Y, Z), f32),
                vm((X, Y, Z), f32),
                vm((X, Y, Z), f32),
                vm((X, Y, Z), f32),
                vm((X + 2, YP, Z), f32),
                vm((max(A, 2), Y, Z), f32),
                vm((2, YC, Z), f32),
                vm((2, YC, Z), f32),
                vm((A, YC, Z), f32),
                vm((A, YC, Z), f32),
                vm((X, Y, Z), f32),
                vm((X, Y, Z), f32),
                vm((CP, CYP, Z), f32),
                vm((CP + 1, YC, Z), f32),
                vm((CP, CYP, Z), f32),
                vm((CP, YC, Z), f32),
                vm((CP, YC, Z), f32),
                vm((CP, YC, Z), f32),
                vm((n_tm, CP, YC, Z), f32),
                vm((n_tm, CP, CYP, Z), f32),
                vm((X + 2, Y, Z), f32),
                dma((3, 2)),
                dma((3, 2)),
                dma((2, 2, T)),
                dma((2, 2, T)),
                dma((2 * H,)),
                dma((2 * H,)),
                dma((2,)),
                dma((2,)),
                dma,
                dma,
                dma((n_tm,)),
                dma((n_tm,)),
                dma((n_tm, 2 * H)),
                dma((n_tm, 2 * H)),
                dma,
                dma,
            ],
            compiler_params=pltpu.CompilerParams(
                collective_id=0, has_side_effects=True, vmem_limit_bytes=60 * 2**20
            ),
        )(source, initial, mobility, labels, electrode, rates)

    return jax.shard_map(
        on_device,
        mesh=mesh,
        in_specs=(
            P("tm", "space", None, None),
            P("space", None, None),
            P("space", None, None),
            P("space", None, None),
            P("space", None, None),
            P(),
        ),
        out_specs=P("tm", "space", None, None),
        check_vma=False,
    )
```

```python
import functools

import jax
import jax.numpy as jnp
from jax import lax
from jax.experimental import pallas as pl
from jax.experimental.pallas import tpu as pltpu
from jax.sharding import PartitionSpec as P

PASSES = 4

source_coef = 0.5
drift_coef = 0.5
react_coef = 0.5
damping = 0.8
coarse_lateral = 0.06
coarse_axial = 0.12

PAD = 8
CHUNK = 16


def kernel(
    n_tm,
    n_space,
    regions,
    source_far,
    initial_far,
    mobility_far,
    labels_far,
    electrode_far,
    rates,
    out_far,
    source,
    initial,
    mobility,
    labels,
    electrode,
    out,
    s_in,
    s_out,
    V,
    IE,
    ME,
    EB,
    F,
    FS,
    KP,
    FR,
    FW,
    FX,
    FY,
    FZ,
    BZ,
    AZ,
    D0,
    W,
    TMP,
    HS,
    HX,
    OS,
    OB,
    VO,
    VS,
    CM,
    GX,
    GY,
    GL,
    GH,
    GD,
    R,
    C,
    UP,
    s_init,
    r_init,
    s_v,
    r_v,
    s_cm,
    r_cm,
    s_hx,
    r_hx,
    s_o,
    r_o,
    s_r,
    r_r,
    s_d,
    r_d,
    s_vo,
    r_vo,
):
    T, X, Y, Z = source.shape
    A, YC = X // 2, Y // 2
    H = -(-n_tm // A)
    E = A * H
    CP = A + 2 * E
    rows = pl.ds(PAD, Y)
    crows = pl.ds(PAD, YC)
    k = lax.axis_index("tm")
    s = lax.axis_index("space")

    def beyond(q, d=1):
        return s >= d if q == 0 else s + d < n_space

    def space_id(q, d=1):
        return {"space": s - d if q == 0 else s + d}

    def remote(src, dst, send, recv, where):
        return pltpu.make_async_remote_copy(
            src_ref=src,
            dst_ref=dst,
            send_sem=send,
            recv_sem=recv,
            device_id=where,
            device_id_type=pl.DeviceIdType.MESH,
        )

    def each_side(action, d=1):
        for q in (0, 1):
            pl.when(beyond(q, d))(functools.partial(action, q))

    barrier = pltpu.get_barrier_semaphore()

    def greet(where):
        pl.semaphore_signal(
            barrier, inc=1, device_id=where, device_id_type=pl.DeviceIdType.MESH
        )

    for d in range(1, H + 1):
        each_side(lambda q, d=d: greet(space_id(q, d)), d)
    for d in range(1, n_tm):
        greet({"tm": lax.rem(k + d, n_tm)})

    fetches = [
        pltpu.make_async_copy(far, near, s_in.at[i])
        for i, (far, near) in enumerate(
            (
                (mobility_far, mobility),
                (initial_far, initial),
                (electrode_far, electrode),
                (labels_far, labels),
                (source_far, source),
            )
        )
    ]
    for fetch in fetches:
        fetch.start()

    edge = jnp.zeros((PAD, Z), jnp.float32)
    plane = jnp.zeros((Y, Z), jnp.float32)
    cplane = jnp.zeros((YC, Z), jnp.float32)
    top, bottom = pl.ds(0, PAD), pl.ds(PAD + Y, PAD)
    ctop, cbottom = pl.ds(0, PAD), pl.ds(PAD + YC, PAD)
    for x in range(X + 2):
        for ref in (IE, ME, W):
            ref[x, top] = edge
            ref[x, bottom] = edge

        def clear(i, carry, x=x):
            for b in (0, 1):
                V[b, i, x, top] = edge
                V[b, i, x, bottom] = edge
            return carry

        lax.fori_loop(1, T + 1, clear, 0)
    for x in range(X):
        FY[x, bottom] = edge
    W[0, rows] = plane
    W[X + 1, rows] = plane

    def clear_coarse(p, carry):
        for ref in (CM, GY):
            ref[p, ctop] = edge
            ref[p, cbottom] = edge
        for j in range(n_tm):
            C[j, p, ctop] = edge
            C[j, p, cbottom] = edge
        return carry

    lax.fori_loop(0, CP, clear_coarse, 0)
    for q in (0, 1):

        @pl.when(jnp.logical_not(beyond(q)))
        def _(q=q):
            x = 0 if q == 0 else X + 1
            IE[x, rows] = plane
            ME[x, rows] = plane
            FR[x] = plane
            HX[q] = cplane

            def clear_halo(i, carry):
                for b in (0, 1):
                    V[b, i, x, rows] = plane
                return carry

            lax.fori_loop(1, T + 1, clear_halo, 0)

        for d in range(1, H + 1):

            @pl.when(jnp.logical_not(beyond(q, d)))
            def _(q=q, d=d):
                for a in range(A):
                    p = E - A * d + a if q == 0 else E + A * d + a
                    CM[p, crows] = cplane
                    for j in range(n_tm):
                        R[j, p] = cplane

    peers = jnp.minimum(s, H) + jnp.minimum(n_space - 1 - s, H) + (n_tm - 1)
    pl.semaphore_wait(barrier, peers)

    def start_copy(item, q):
        src, dst = ((initial_far, IE), (mobility_far, ME), (electrode_far, EB))[item]
        x = 0 if q == 0 else X - 1
        if item < 2:
            target = dst.at[X + 1 if q == 0 else 0, rows]
        else:
            target = dst.at[1 - q]
        return remote(src.at[x], target, s_init.at[item, q], r_init.at[item, 1 - q], space_id(q))

    def landed(item, q):
        src, dst = ((initial_far, IE), (mobility_far, ME), (electrode_far, EB))[item]
        if item < 2:
            target = dst.at[0 if q == 0 else X + 1, rows]
        else:
            target = dst.at[q]
        return remote(src.at[0], target, s_init.at[item, q], r_init.at[item, q], space_id(q))

    for item in (1, 0, 2):
        each_side(lambda q, item=item: start_copy(item, q).start())

    for fetch in fetches[:2]:
        fetch.wait()
    for x in range(X):
        IE[x + 1, rows] = initial[x]
        ME[x + 1, rows] = mobility[x]
        for b in (0, 1):
            V[b, 0, x + 1, rows] = initial[x]

    def pair_rows(value, slot):
        TMP[slot] = value
        return TMP[slot, pl.ds(0, YC, stride=2), :] + TMP[slot, pl.ds(1, YC, stride=2), :]

    for a in range(A):
        CM[E + a, crows] = 0.25 * pair_rows(mobility[2 * a] + mobility[2 * a + 1], a)

    def reach(j, d):
        return min(A, n_tm - j - A * (d - 1))

    def deep(ref, pick, j, q, d, send, recv, incoming):
        n = reach(j, d)
        mine = E if q == 0 else E + A - n
        if incoming:
            there = E - A * d + A - n if q == 0 else E + A * d
        else:
            there = E + A * d if q == 0 else E - A * d + A - n
        slot = 2 * (d - 1)
        return remote(
            pick(ref, mine, n),
            pick(ref, there, n),
            send(slot + q),
            recv(slot + (q if incoming else 1 - q)),
            space_id(q, d),
        )

    def cm_copy(q, d, incoming):
        return deep(
            CM,
            lambda ref, p, n: ref.at[pl.ds(p, n), crows],
            0,
            q,
            d,
            lambda i: s_cm.at[i],
            lambda i: r_cm.at[i],
            incoming,
        )

    for d in range(1, H + 1):
        each_side(lambda q, d=d: cm_copy(q, d, False).start(), d)

    for fetch in fetches[2:]:
        fetch.wait()
    lane = lax.broadcasted_iota(jnp.int32, (Y, Z), 1)
    not_first, not_last = lane > 0, lane < Z - 1

    def half_forcing(t, carry):
        for x in range(X):
            F[t, x] = source_coef * source[t, x]
        return carry

    lax.fori_loop(0, T, half_forcing, 0)
    for x in range(X):
        total = F[0, x]
        for t in range(1, T):
            total = total + F[t, x]
        FS[x] = total
        lab = labels[x]
        rate = jnp.zeros((Y, Z), jnp.float32)
        for i in range(regions):
            rate = jnp.where(lab == i, rates[i], rate)
        KP[x] = react_coef * rate
        free = 1.0 - electrode[x].astype(jnp.float32)
        FR[x + 1] = free
        FW[x] = damping * free
        mid = mobility[x]
        FY[x, rows] = 0.5 * (mid + ME[x + 1, pl.ds(PAD - 1, Y)])
        FY[x, pl.ds(PAD + Y, 1)] = 0.5 * mobility[x, pl.ds(Y - 1, 1)]
        low = 0.5 * (mid + jnp.where(not_first, pltpu.roll(mid, 1, 1), 0.0))
        high = 0.5 * (mid + jnp.where(not_last, pltpu.roll(mid, Z - 1, 1), 0.0))
        BZ[x] = jnp.where(not_first, (1.0 + drift_coef) * low, 0.0)
        AZ[x] = jnp.where(not_last, high, 0.0)
        FZ[x] = FY[x, pl.ds(PAD + 1, Y)]
        D0[x] = 1.0 + low + (1.0 + drift_coef) * high + FY[x, rows] + FY[x, pl.ds(PAD + 1, Y)]
    for x in range(1, X):
        FX[x] = 0.5 * (mobility[x - 1] + mobility[x])

    @pl.when(k == 0)
    def _():
        for a in range(A):
            OB[a] = pair_rows(initial[2 * a] + initial[2 * a + 1], a)

    each_side(lambda q: landed(1, q).wait_recv())
    FX[0] = 0.5 * (ME[0, rows] + ME[1, rows])
    FX[X] = 0.5 * (ME[X, rows] + ME[X + 1, rows])
    for x in range(X):
        D0[x] = D0[x] + FX[x] + FX[x + 1]

    def around(read, x, centre, r=0, n=Y):
        i = x - 1
        here = pl.ds(r, n)
        return (
            FX[i, here] * read(x - 1, PAD + r)
            + FX[i + 1, here] * read(x + 1, PAD + r)
            + FY[i, pl.ds(PAD + r, n)] * read(x, PAD + r - 1)
            + FZ[i, here] * read(x, PAD + r + 1)
            + BZ[i, here] * pltpu.roll(centre, 1, 1)
            + AZ[i, here] * pltpu.roll(centre, Z - 1, 1)
        )

    def v_copy(b, t, q):
        x = 1 if q == 0 else X
        there = X + 1 if q == 0 else 0
        return remote(
            V.at[b, t + 1, x, rows],
            V.at[b, t + 1, there, rows],
            s_v.at[b, q, t],
            r_v.at[b, 1 - q, t],
            space_id(q),
        )

    def v_landed(b, t, q):
        x = 0 if q == 0 else X + 1
        return remote(
            V.at[b, t + 1, 1, rows],
            V.at[b, t + 1, x, rows],
            s_v.at[b, q, t],
            r_v.at[b, q, t],
            space_id(q),
        )

    each_side(lambda q: landed(0, q).wait_recv())

    def first_plane(x):
        i = x - 1
        now = IE[x, rows]
        half = KP[i] * jnp.abs(now)
        part = D0[i] + half
        common = around(lambda xx, o: IE[xx, pl.ds(o, Y)], x, now) + now - now * part
        TMP[0] = common
        TMP[1] = FW[i] / (part + half)

        def step(index, carry):
            t = T - 1 - index
            V[1, t + 1, x, rows] = IE[x, rows] + TMP[1] * (F[t, i] + TMP[0])
            if x in (1, X):
                q = 0 if x == 1 else 1
                pl.when(beyond(q))(lambda: v_copy(1, t, q).start())
            return carry

        lax.fori_loop(0, T, step, 0)

    for x in (1, X) + tuple(range(2, X)):
        first_plane(x)

    def relaxed(b, t, x, r, n):
        i = x - 1
        here, mine = pl.ds(r, n), pl.ds(PAD + r, n)
        now = V[b, t + 1, x, mine]
        half = KP[i, here] * jnp.abs(now)
        part = D0[i, here] + half
        gain = (
            around(lambda xx, o: V[b, t + 1, xx, pl.ds(o, n)], x, now, r, n)
            + (F[t, i, here] + V[b, t, x, mine])
            - now * part
        )
        return now + FW[i, here] * gain / (part + half)

    def one_pass(
        b, arriving, sending, free_send, last, after_ends=None, after_last=None, before_first=None
    ):
        o = 1 - b

        def store(t, x):
            for r in range(0, Y, CHUNK):
                value = relaxed(b, t, x, r, CHUNK)
                if last:
                    out[t, x - 1, pl.ds(r, CHUNK)] = value
                else:
                    V[o, t + 1, x, pl.ds(PAD + r, CHUNK)] = value

        def leave(t):
            return pltpu.make_async_copy(out.at[t], out_far.at[t], s_out.at[t])

        def ends(index, carry):
            t = T - 1 - index
            if arriving:
                each_side(lambda q: v_landed(b, t, q).wait_recv())
            if free_send:
                each_side(lambda q: v_copy(o, t, q).wait_send())
            for q, x in ((0, 1), (1, X)):
                store(t, x)
            if sending:
                each_side(lambda q: v_copy(o, t, q).start())
            return carry

        def inner(index, carry):
            t = T - 1 - index
            for x in range(2, X):
                store(t, x)
            if last:
                leave(t).start()
            return carry

        def step(index, carry):
            return inner(index, ends(index, carry))

        if after_ends is not None:
            lax.fori_loop(0, T, ends, 0)
            after_ends()
            inner(0, 0)
            after_last()
            lax.fori_loop(1, T, inner, 0)
        elif before_first is not None:
            lax.fori_loop(0, T - 1, step, 0)
            before_first()
            lax.fori_loop(T - 1, T, step, 0)
        else:
            lax.fori_loop(0, T, step, 0)
        if last:
            for t in range(T):
                leave(t).wait()

    g = PASSES % 2

    def total_of(x):
        total = V[g, 1, x, rows]
        for t in range(1, T):
            total = total + V[g, t + 1, x, rows]
        return total

    def hx_copy(q):
        return remote(HS.at[q], HX.at[1 - q], s_hx.at[q], r_hx.at[1 - q], space_id(q))

    def hx_landed(q):
        return remote(HS.at[q], HX.at[q], s_hx.at[q], r_hx.at[q], space_id(q))

    def send_faces():
        for q, x in ((0, 1), (1, X)):
            total = total_of(x)
            W[x, rows] = total
            HS[q] = 0.25 * pair_rows(FX[0 if q == 0 else X] * total, q)
        each_side(lambda q: hx_copy(q).start())

        def v_out(index, carry):
            each_side(lambda q: v_copy(g, T - 1 - index, q).start())
            return carry

        lax.fori_loop(0, T, v_out, 0)

    o_copy = remote(OS, OB, s_o, r_o, {"tm": lax.rem(k + 1, n_tm)})
    vo_copy = remote(VS, VO, s_vo, r_vo, {"tm": lax.rem(k + 1, n_tm)})

    def send_last():
        for a in range(A):
            OS[a] = pair_rows(V[g, T, 2 * a + 1, rows] + V[g, T, 2 * a + 2, rows], a)
        for x in range(X):
            VS[x] = V[g, T, x + 1, rows]

        @pl.when(k < n_tm - 1)
        def _():
            o_copy.start()

    for number in range(2, PASSES):
        one_pass((number + 1) % 2, True, True, number > 2, False)
    one_pass((PASSES + 1) % 2, True, False, PASSES > 2, False, send_faces, send_last)

    for x in range(2, X):
        W[x, rows] = total_of(x)

    def residual_sum(x):
        i = x - 1
        total = W[x, rows]
        quad = jnp.zeros((Y, Z), jnp.float32)
        for t in range(T):
            value = V[g, t + 1, x, rows]
            quad = quad + value * jnp.abs(value)
        return (
            FS[i]
            + (total - V[g, T, x, rows])
            + around(lambda xx, o: W[xx, pl.ds(o, Y)], x, total)
            - D0[i] * total
            - KP[i] * quad
        )

    own = []
    for a in range(A):
        own.append(pair_rows(residual_sum(2 * a + 1) + residual_sum(2 * a + 2), a))

    @pl.when(k > 0)
    def _():
        o_copy.wait_recv()

    each_side(lambda q: hx_landed(q).wait_recv())
    for a in range(A):
        value = 0.25 * (own[a] + OB[a])
        if a == 0:
            value = value + HX[0]
        if a == A - 1:
            value = value + HX[1]
        R[k, E + a] = value

    def r_copy(d):
        return remote(
            R.at[k, pl.ds(E, A)],
            R.at[k, pl.ds(E, A)],
            s_r.at[d],
            r_r.at[k],
            {"tm": lax.rem(k + d, n_tm)},
        )

    def r_landed(j):
        return remote(
            R.at[j, pl.ds(E, A)],
            R.at[j, pl.ds(E, A)],
            s_r.at[0],
            r_r.at[j],
            {"tm": lax.rem(k + 1, n_tm)},
        )

    for d in range(n_tm - 1, 0, -1):
        r_copy(d).start()

    @pl.when(k < n_tm - 1)
    def _():
        vo_copy.start()

    for d in range(1, H + 1):
        each_side(lambda q, d=d: cm_copy(q, d, True).wait_recv(), d)
    clane = lax.broadcasted_iota(jnp.int32, (YC, Z), 1)
    c_first, c_last = clane > 0, clane < Z - 1
    lo = E - (n_tm - 1)
    hi = E + A + (n_tm - 1)

    def coarse_faces(p, carry):
        GX[p] = (0.5 * coarse_lateral) * (CM[p - 1, crows] + CM[p, crows])
        return carry

    lax.fori_loop(lo, hi + 1, coarse_faces, 0)

    def coarse_coefs(p, carry):
        mid = CM[p, crows]
        near = (0.5 * coarse_lateral) * (mid + CM[p, pl.ds(PAD - 1, YC)])
        far = (0.5 * coarse_lateral) * (mid + CM[p, pl.ds(PAD + 1, YC)])
        GY[p, crows] = near
        low = (0.5 * coarse_axial) * (
            mid + jnp.where(c_first, pltpu.roll(mid, 1, 1), 0.0)
        )
        high = (0.5 * coarse_axial) * (
            mid + jnp.where(c_last, pltpu.roll(mid, Z - 1, 1), 0.0)
        )
        GL[p] = jnp.where(c_first, low, 0.0)
        GH[p] = jnp.where(c_last, high, 0.0)
        GD[p] = 1.0 - (GX[p] + GX[p + 1] + near + far + low + high)
        return carry

    lax.fori_loop(lo, hi, coarse_coefs, 0)

    def d_copy(j, q, d, incoming):
        return deep(
            R,
            lambda ref, p, n: ref.at[j, pl.ds(p, n)],
            j,
            q,
            d,
            lambda i: s_d.at[j, i],
            lambda i: r_d.at[j, i],
            incoming,
        )

    def distances(j):
        return [d for d in range(1, H + 1) if reach(j, d) > 0]

    for j in range(n_tm):
        pl.when(k != j)(lambda j=j: r_landed(j).wait_recv())
        for d in distances(j):
            each_side(lambda q, d=d, j=j: d_copy(j, q, d, False).start(), d)

    for j in range(n_tm):
        for d in distances(j):
            each_side(lambda q, d=d, j=j: d_copy(j, q, d, True).wait_recv(), d)

        def coarse_plane(p, carry, j=j):
            if j == 0:
                C[0, p, crows] = R[0, p]
                return carry
            mid = C[j - 1, p, crows]
            value = (
                R[j, p]
                + GD[p] * mid
                + GX[p] * C[j - 1, p - 1, crows]
                + GX[p + 1] * C[j - 1, p + 1, crows]
                + GY[p, crows] * C[j - 1, p, pl.ds(PAD - 1, YC)]
                + GY[p, pl.ds(PAD + 1, YC)] * C[j - 1, p, pl.ds(PAD + 1, YC)]
                + GL[p] * pltpu.roll(mid, 1, 1)
                + GH[p] * pltpu.roll(mid, Z - 1, 1)
            )
            where = A * s + p - E
            inside = jnp.logical_and(where >= 0, where < A * n_space)
            C[j, p, crows] = jnp.where(inside, value, 0.0)
            return carry

        width = n_tm - j
        lax.fori_loop(E - width, E + A + width, coarse_plane, 0, unroll=2)

    each_side(lambda q: landed(2, q).wait_recv())
    for q in (0, 1):

        @pl.when(beyond(q))
        def _(q=q):
            FR[0 if q == 0 else X + 1] = 1.0 - EB[q].astype(jnp.float32)

    def spread(j, x):
        value = C[j, E + (x + 1) // 2 - 1, crows]
        UP[x, pl.ds(0, YC, stride=2), :] = value
        UP[x, pl.ds(1, YC, stride=2), :] = value
        return FR[x] * UP[x]

    def v_home(t, carry):
        each_side(lambda q: v_copy(g, t, q).wait_send())
        each_side(lambda q: v_landed(g, t, q).wait_recv())
        return carry

    lax.fori_loop(0, T, v_home, 0)

    for x in range(X + 2):
        move = spread(k, x)
        for t in range(T):
            V[g, t + 1, x, rows] = V[g, t + 1, x, rows] + move

    def open_sweep():
        @pl.when(k > 0)
        def _():
            vo_copy.wait_recv()
            for x in range(1, X + 1):
                opening = VO[x - 1] + spread(k - 1, x)
                for b in (0, 1):
                    V[b, 0, x, rows] = opening

    for number in range(1, PASSES + 1):
        one_pass(
            (g + number + 1) % 2,
            number > 1,
            number < PASSES,
            number in (1, 3),
            number == PASSES,
            before_first=open_sweep if number == 1 else None,
        )

    def drain(t, carry):
        for b in (0, 1):
            each_side(lambda q, b=b: v_copy(b, t, q).wait_send())
        return carry

    lax.fori_loop(0, T, drain, 0)
    for item in range(3):
        each_side(lambda q, item=item: start_copy(item, q).wait_send())
    each_side(lambda q: hx_copy(q).wait_send())
    for d in range(1, H + 1):
        each_side(lambda q, d=d: cm_copy(q, d, False).wait_send(), d)
    for j in range(n_tm):
        for d in distances(j):
            each_side(lambda q, d=d, j=j: d_copy(j, q, d, False).wait_send(), d)
    for d in range(1, n_tm):
        r_copy(d).wait_send()

    @pl.when(k < n_tm - 1)
    def _():
        o_copy.wait_send()
        vo_copy.wait_send()


def solution(mesh):
    n_tm, n_space = mesh.shape["tm"], mesh.shape["space"]

    def on_device(source, initial, mobility, labels, electrode, rates):
        T, X, Y, Z = source.shape
        A, YC = X // 2, Y // 2
        H = -(-n_tm // A)
        CP = A + 2 * A * H
        YP, CYP = Y + 2 * PAD, YC + 2 * PAD
        f32 = jnp.float32
        vm = pltpu.VMEM
        dma = pltpu.SemaphoreType.DMA
        in_hbm = pl.BlockSpec(memory_space=pltpu.HBM)
        return pl.pallas_call(
            functools.partial(kernel, n_tm, n_space, rates.shape[0]),
            out_shape=jax.ShapeDtypeStruct(source.shape, f32),
            in_specs=[in_hbm] * 5 + [pl.BlockSpec(memory_space=pltpu.SMEM)],
            out_specs=in_hbm,
            scratch_shapes=[
                vm((T, X, Y, Z), f32),
                vm((X, Y, Z), f32),
                vm((X, Y, Z), f32),
                vm((X, Y, Z), jnp.int32),
                vm((X, Y, Z), jnp.int32),
                vm((T, X, Y, Z), f32),
                dma((5,)),
                dma((T,)),
                vm((2, T + 1, X + 2, YP, Z), f32),
                vm((X + 2, YP, Z), f32),
                vm((X + 2, YP, Z), f32),
                vm((2, Y, Z), jnp.int32),
                vm((T, X, Y, Z), f32),
                vm((X, Y, Z), f32),
                vm((X, Y, Z), f32),
                vm((X + 2, Y, Z), f32),
                vm((X, Y, Z), f32),
                vm((X + 1, Y, Z), f32),
                vm((X, YP, Z), f32),
                vm((X, Y, Z), f32),
                vm((X, Y, Z), f32),
                vm((X, Y, Z), f32),
                vm((X, Y, Z), f32),
                vm((X + 2, YP, Z), f32),
                vm((max(A, 2), Y, Z), f32),
                vm((2, YC, Z), f32),
                vm((2, YC, Z), f32),
                vm((A, YC, Z), f32),
                vm((A, YC, Z), f32),
                vm((X, Y, Z), f32),
                vm((X, Y, Z), f32),
                vm((CP, CYP, Z), f32),
                vm((CP + 1, YC, Z), f32),
                vm((CP, CYP, Z), f32),
                vm((CP, YC, Z), f32),
                vm((CP, YC, Z), f32),
                vm((CP, YC, Z), f32),
                vm((n_tm, CP, YC, Z), f32),
                vm((n_tm, CP, CYP, Z), f32),
                vm((X + 2, Y, Z), f32),
                dma((3, 2)),
                dma((3, 2)),
                dma((2, 2, T)),
                dma((2, 2, T)),
                dma((2 * H,)),
                dma((2 * H,)),
                dma((2,)),
                dma((2,)),
                dma,
                dma,
                dma((n_tm,)),
                dma((n_tm,)),
                dma((n_tm, 2 * H)),
                dma((n_tm, 2 * H)),
                dma,
                dma,
            ],
            compiler_params=pltpu.CompilerParams(
                collective_id=0, has_side_effects=True, vmem_limit_bytes=60 * 2**20
            ),
        )(source, initial, mobility, labels, electrode, rates)

    return jax.shard_map(
        on_device,
        mesh=mesh,
        in_specs=(
            P("tm", "space", None, None),
            P("space", None, None),
            P("space", None, None),
            P("space", None, None),
            P("space", None, None),
            P(),
        ),
        out_specs=P("tm", "space", None, None),
        check_vma=False,
    )
```
